256 devices in a mesh: leaf: 4 (over y), dom: 64 (over x, z, core).
Axes of the slice: x: 4, y: 4, z: 8, core: 2. Of those that a mesh axis runs over, the one named last changes fastest.
Arguments:
- parent_coords: float32 [3, 125, 8192], P(None, None, ('leaf', 'dom')), may hold values from -1.8 to 1.8
- coarse_coords: float32 [3, 125, 65536], P(None, None, ('leaf', 'dom')), may hold values from -1.8 to 1.8
- child_parent: int32 [65536], P(('leaf', 'dom')), may hold values from -1 to 31, as said below
- child_octant: int32 [65536], P(('leaf', 'dom')), may hold values from 0 to 7
- face_elem: int32 [65536], P(('leaf', 'dom')), may hold values from 0 to 255
- face_side: int32 [65536], P(('leaf', 'dom')), may hold values from 0 to 5
- face_owner: int32 [65536, 1], P(('leaf', 'dom')), may hold values from 0 to 255; in each aligned block of 256 rows (0 to 255, 256 to 511, ...) at most 2 rows name the same one
- coarse_elem: int32 [65536], P(('leaf', 'dom')), may hold values from 0 to 255
- coarse_side: int32 [65536], P(('leaf', 'dom')), may hold values from 0 to 5
- quadrant: int32 [65536], P(('leaf', 'dom')), may hold values from 0 to 3
Outputs:
- jac_det: float32 [125, 65536], P(None, ('leaf', 'dom'))
- face_normals: float32 [3, 25, 65536], P(None, None, ('leaf', 'dom'))
- coarse_partials: float32 [3, 150, 65536], P(None, None, ('leaf', 'dom'))
The draws below stay inside these ranges and needn't reach their ends.
Inputs may be any that keep to these rules, and one draw needn't show every extreme that they name: `face_owner`: the rows of one device (aligned blocks of 256 records) name one owner at most 2 times; some owner is named exactly 2 times. `child_parent`: -1 names the last parent of the previous device block; the first device block has no -1; values never fall within a block.
All inputs are finite; a program needn't handle non-finite values.
Results may differ from the reference program's by a relative error of at most 0.0003.
Values sent between devices are 32-bit elements; how exact they have to be, the bound alone decides.
A program may use at most 128 MiB of HBM per device.

```python
import math
import jax
import jax.numpy as jnp
import numpy as np
from jax import lax

NODES = 125
E_DEV = 256
F_DEV = 256
KC = 256
RANKS = 256
CAP = 2
PAR = 32
ELEMS = 65536
PARENTS = 8192
COARSE = 65536
FACES = 65536


def child_layout(key):
    inner = jax.random.fold_in(key, 7)
    shifts = jax.random.randint(inner, (ELEMS // E_DEV,), 1, 8)
    ranks_order = jnp.arange(ELEMS // E_DEV, dtype=jnp.int32)
    shifts = jnp.where(ranks_order == 0, 0, shifts).astype(jnp.int32)
    rows = jnp.arange(ELEMS, dtype=jnp.int32)
    device_shift = shifts[rows // E_DEV]
    offset = rows % E_DEV - device_shift
    parent = jnp.where(offset < 0, -1, offset // 8)
    octant = jnp.where(offset < 0, offset + 8, offset % 8)
    return (parent.astype(jnp.int32), octant.astype(jnp.int32))


def draw_child_parent(key, part):
    return child_layout(key)[0]


def draw_child_octant(key, part):
    return child_layout(key)[1]


def plant(entries, stream_key, low, high):
    longest = entries.shape.index(max(entries.shape))
    spots = []
    for shift in (0, 1):
        where = [jax.random.randint(jax.random.fold_in(stream_key, axis), (), 0, length) for axis, length in enumerate(entries.shape)]
        where[longest] = (where[longest] + shift) % entries.shape[longest]
        spots.append(tuple(where))
    return entries.at[spots[0]].set(low).at[spots[1]].set(high)


def levels(rng, extent, split, low, top_value):
    gain = 1.0
    for position, parts in split:
        draws = jax.random.uniform(jax.random.fold_in(jax.random.fold_in(rng, 6), position), (parts,), jnp.float32, low / len(split), top_value / len(split))
        gain = gain * jnp.repeat(jnp.exp(draws), extent[position] // parts).reshape((-1,) + (1,) * (len(extent) - 1 - position))
    return gain


def assign_block(stream_key, own, number, rows, amount, top, limit, skew):
    ranking = jax.random.permutation(stream_key, amount)
    crowded, usual = shares(amount, rows * top, limit, skew, True), shares(amount, rows * top, limit, skew, False)
    places = jnp.arange(amount)

    def named(lengths, turn):
        used = int((lengths > 0).sum())
        fixed = max(1, used // 4)
        shifted = fixed + (places - fixed + turn * (used - fixed)) % max(1, amount - fixed)
        return jnp.zeros((amount,), jnp.int32).at[ranking[jnp.where(places < fixed, places, shifted)]].set(jnp.asarray(lengths, jnp.int32))

    lengths = jnp.where(number % 4 == 0, named(crowded, number // 4), named(usual, number - number // 4 - 1))
    mixed = jax.random.permutation(jax.random.fold_in(own, 3), amount)
    giver, receiver = mixed[0:amount // 2 * 2:2], mixed[1:amount // 2 * 2:2]
    room = jnp.minimum(lengths[giver] - 1, limit - lengths[receiver]) // 2
    room = jnp.where((giver == ranking[0]) | (receiver == ranking[0]) | (lengths[receiver] == 0), 0, jnp.maximum(room, 0))
    shifted = jax.random.randint(jax.random.fold_in(own, 4), (amount // 2,), 0, 1 << 20) % (room + 1)
    lengths = lengths.at[giver].add(-shifted).at[receiver].add(shifted)
    members = jnp.searchsorted(jnp.cumsum(lengths), jnp.arange(rows * top), side="right").astype(jnp.int32)
    table = members.reshape(top, rows).T
    table = table[jax.random.permutation(jax.random.fold_in(own, 1), rows)]
    turn = jax.random.randint(jax.random.fold_in(own, 2), (rows, 1), 0, top)
    return jnp.take_along_axis(table, (jnp.arange(top)[None, :] + turn) % top, axis=1)


def shares(amount, total, reach, skew, full):
    portions = [(1 << 20) // math.isqrt(standing ** skew) + 1 for standing in range(1, amount + 1)]
    largest = reach if full else min(reach, max(-(-total // amount), total * portions[0] // sum(portions)))
    least = 1 if total - largest >= amount - 1 else 0
    given, rest = [largest] + [least] * (amount - 1), total - largest - least * (amount - 1)
    while rest > 0:
        movable = [i for i in range(1, amount) if given[i] < largest] or [i for i in range(1, amount) if given[i] < reach]
        mass, remaining = sum([portions[i] for i in movable]), rest
        for i in movable:
            more = min(reach - given[i], max(1, remaining * portions[i] // mass), rest)
            given[i] = given[i] + more
            rest = rest - more
    return np.array(given)


def scatter_about(key, extent, spread, limit, split=(), kind=jnp.bfloat16):
    entries = spread * jax.random.normal(key, extent, jnp.float32)
    if split:
        entries = entries * levels(key, extent, split, -0.22, 0.18)
    return jnp.clip(entries, -limit, limit).astype(kind)


def setup_inputs(seed: int = 0) -> dict:
    splits = jax.random.split(jax.random.key(seed), 11)
    parent_coords = scatter_about(splits[0], (3, NODES, PARENTS), 0.3, 1.8, ((2, 256),), jnp.float32)
    coarse_coords = scatter_about(splits[1], (3, NODES, COARSE), 0.3, 1.8, ((2, 256),), jnp.float32)
    child_parent = draw_child_parent(jax.random.fold_in(splits[10], 71), 0)
    child_octant = draw_child_octant(jax.random.fold_in(splits[10], 71), 0)
    face_elem = plant(jax.random.randint(splits[4], (FACES,), 0, E_DEV), jax.random.fold_in(splits[4], 1), 0, E_DEV - 1).astype(jnp.int32)
    face_side = plant(jax.random.randint(splits[5], (FACES,), 0, 6), jax.random.fold_in(splits[5], 1), 0, 5).astype(jnp.int32)
    face_owner_keys = jax.random.split(jax.random.fold_in(splits[6], 1), FACES // F_DEV)
    face_owner_turns = jax.random.permutation(jax.random.fold_in(splits[6], 3), FACES // F_DEV)
    face_owner = jax.vmap(lambda own, number: assign_block(jax.random.fold_in(splits[6], 2), own, number, F_DEV, RANKS, 1, CAP, 2))(face_owner_keys, face_owner_turns).reshape((FACES, 1))
    coarse_elem = plant(jax.random.randint(splits[7], (FACES,), 0, KC), jax.random.fold_in(splits[7], 1), 0, KC - 1).astype(jnp.int32)
    coarse_side = plant(jax.random.randint(splits[8], (FACES,), 0, 6), jax.random.fold_in(splits[8], 1), 0, 5).astype(jnp.int32)
    quadrant = plant(jax.random.randint(splits[9], (FACES,), 0, 4), jax.random.fold_in(splits[9], 1), 0, 3).astype(jnp.int32)
    return dict(parent_coords=parent_coords, coarse_coords=coarse_coords, child_parent=child_parent, child_octant=child_octant, face_elem=face_elem, face_side=face_side, face_owner=face_owner, coarse_elem=coarse_elem, coarse_side=coarse_side, quadrant=quadrant)


def lobatto_nodes():
    return np.array([-1.0, -math.sqrt(3.0 / 7.0), 0.0, math.sqrt(3.0 / 7.0), 1.0])

def lagrange_table(targets):
    points = lobatto_nodes()
    table = np.ones((targets.shape[0], 5))
    for column in range(5):
        for others in range(5):
            if others != column:
                table[:, column] *= (targets - points[others]) / (points[column] - points[others])
    return table

def derivative_table():
    points = lobatto_nodes()
    table = np.zeros((5, 5))
    for target in range(5):
        for column in range(5):
            total = 0.0
            for others in range(5):
                if others != column:
                    term = 1.0 / (points[column] - points[others])
                    for remain in range(5):
                        if remain != column and remain != others:
                            term *= (points[target] - points[remain]) / (points[column] - points[remain])
                    total += term
            table[target, column] = total
    return table

def lower_table():
    return lagrange_table((lobatto_nodes() - 1.0) / 2.0)

def upper_table():
    return lagrange_table((lobatto_nodes() + 1.0) / 2.0)

def apply_axis(table, field, axis):
    moved = jnp.tensordot(jnp.asarray(table, jnp.float32), field, axes=((1,), (axis,)), precision=lax.Precision.HIGHEST)
    return jnp.moveaxis(moved, 0, axis)

def halves(field, axis, choose, lower, upper):
    return jnp.where(choose, apply_axis(upper, field, axis), apply_axis(lower, field, axis))

def build_children(parents, octant):
    field = parents
    lower, upper = (lower_table(), upper_table())
    for axis, weight in ((1, 4), (2, 2), (3, 1)):
        field = halves(field, axis, octant // weight % 2 == 1, lower, upper)
    return field

def jacobian_det(field):
    slope = derivative_table()
    grads = [apply_axis(slope, field, axis) for axis in (1, 2, 3)]
    first = grads[0][0] * (grads[1][1] * grads[2][2] - grads[2][1] * grads[1][2])
    second = grads[1][0] * (grads[0][1] * grads[2][2] - grads[2][1] * grads[0][2])
    third = grads[2][0] * (grads[0][1] * grads[1][2] - grads[1][1] * grads[0][2])
    return (first - second + third).reshape(125, -1)

def face_nodes(side):
    direction = side // 2
    level = side % 2 * 4
    fixed_stride = jnp.where(direction == 0, 25, jnp.where(direction == 1, 5, 1))
    first_stride = jnp.where(direction == 0, 5, 25)
    second_stride = jnp.where(direction == 2, 5, 1)
    places = jnp.arange(25, dtype=jnp.int32)[:, None]
    nodes = level * fixed_stride + places // 5 * first_stride + places % 5 * second_stride
    return nodes.astype(jnp.int32)

def face_values(field, elements, side):
    return field[:, face_nodes(side), elements[None, :]].reshape(3, 5, 5, -1)

def mortar(fine, coarse, quadrant):
    lower, upper, slope = (lower_table(), upper_table(), derivative_table())
    upper_first = quadrant // 2 == 1
    upper_second = quadrant % 2 == 1
    placed = halves(halves(coarse, 1, upper_first, lower, upper), 2, upper_second, lower, upper)
    merged = 0.5 * (fine + placed)
    along_first = apply_axis(slope, merged, 1)
    along_second = apply_axis(slope, merged, 2)
    normal = jnp.stack([along_first[1] * along_second[2] - along_first[2] * along_second[1], along_first[2] * along_second[0] - along_first[0] * along_second[2], along_first[0] * along_second[1] - along_first[1] * along_second[0]])
    back = halves(normal, 2, upper_second, lower.T, upper.T)
    back = halves(back, 1, upper_first, lower.T, upper.T)
    return (normal, back)

def accumulate(back, element_key, segments):
    data = back.reshape(75, -1).T
    total = jax.ops.segment_sum(data, element_key, num_segments=segments)
    return total.reshape(-1, 6, 3, 25).transpose(2, 1, 3, 0).reshape(3, 150, -1)

def reference(parent_coords, coarse_coords, child_parent, child_octant, face_elem, face_side, face_owner, coarse_elem, coarse_side, quadrant):

    def one_rank(rank):
        parents_local = lax.dynamic_slice_in_dim(child_parent, rank * E_DEV, E_DEV)
        octants = lax.dynamic_slice_in_dim(child_octant, rank * E_DEV, E_DEV)
        index = (rank * PAR + parents_local).astype(jnp.int32)
        gathered = parent_coords[:, :, index].reshape(3, 5, 5, 5, E_DEV)
        children = build_children(gathered, octants)
        determinant = jacobian_det(children)
        elements = lax.dynamic_slice_in_dim(face_elem, rank * F_DEV, F_DEV)
        sides = lax.dynamic_slice_in_dim(face_side, rank * F_DEV, F_DEV)
        fine = face_values(children.reshape(3, 125, E_DEV), elements, sides)
        return (determinant, fine)
    determinants, fines = lax.map(one_rank, jnp.arange(RANKS, dtype=jnp.int32))
    jac_det = determinants.transpose(1, 0, 2).reshape(125, ELEMS)
    fine_all = fines.transpose(1, 2, 3, 0, 4).reshape(3, 5, 5, FACES)
    owner = face_owner[:, 0]
    global_coarse = (owner * KC + coarse_elem).astype(jnp.int32)
    coarse = face_values(coarse_coords, global_coarse, coarse_side)
    normal, back = mortar(fine_all, coarse, quadrant)
    face_normals = normal.reshape(3, 25, FACES)
    coarse_partials = accumulate(back, (global_coarse * 6 + coarse_side).astype(jnp.int32), COARSE * 6)
    return (jac_det, face_normals, coarse_partials)
```

```python
import functools
import math

import jax
import jax.numpy as jnp
import ml_dtypes
import numpy as np
from jax import lax
from jax.experimental import pallas as pl
from jax.experimental.pallas import tpu as pltpu
from jax.sharding import PartitionSpec as P

F32 = jnp.float32
BF16 = jnp.bfloat16
POOL = 40
MIDDLE = 62
VALID, ELEM, SIDE, QUAD, FSIDE, PROW, OCT = 75, 76, 77, 78, 80, 81, 82


def lobatto_nodes():
    return np.array([-1.0, -math.sqrt(3.0 / 7.0), 0.0, math.sqrt(3.0 / 7.0), 1.0])


def lagrange_table(targets):
    points = lobatto_nodes()
    table = np.ones((targets.shape[0], 5))
    for column in range(5):
        for others in range(5):
            if others != column:
                table[:, column] *= (targets - points[others]) / (points[column] - points[others])
    return table


def derivative_table():
    points = lobatto_nodes()
    table = np.zeros((5, 5))
    for target in range(5):
        for column in range(5):
            total = 0.0
            for others in range(5):
                if others != column:
                    term = 1.0 / (points[column] - points[others])
                    for remain in range(5):
                        if remain != column and remain != others:
                            term *= (points[target] - points[remain]) / (
                                points[column] - points[remain]
                            )
                    total += term
            table[target, column] = total
    return table


def f32_table(table):
    return table.astype(np.float32).astype(np.float64)


LOWER = f32_table(lagrange_table((lobatto_nodes() - 1.0) / 2.0))
UPPER = f32_table(lagrange_table((lobatto_nodes() + 1.0) / 2.0))
SLOPE = f32_table(derivative_table())
EYE = np.eye(5)


def halves_of(table):
    high = table.astype(np.float32).astype(ml_dtypes.bfloat16)
    low = (table - high.astype(np.float64)).astype(np.float32).astype(ml_dtypes.bfloat16)
    return high, low


def side_nodes(side):
    direction, level = side // 2, side % 2 * 4
    fixed = (25, 5, 1)[direction]
    first = 5 if direction == 0 else 25
    second = 5 if direction == 2 else 1
    return [level * fixed + a * first + b * second for a in range(5) for b in range(5)]


def child_constant():
    table = np.zeros((128, 8 * 128))
    for octant in range(8):
        picks = [UPPER if octant & bit else LOWER for bit in (4, 2, 1)]
        whole = np.kron(np.kron(picks[0], picks[1]), picks[2])
        table[:125, octant * 128 : octant * 128 + 125] = whole.T
    return np.concatenate(halves_of(table), axis=0)


def slope_constant():
    table = np.zeros((384, 128))
    for direction in range(3):
        picks = [SLOPE if axis == direction else EYE for axis in range(3)]
        whole = np.kron(np.kron(picks[0], picks[1]), picks[2])
        table[direction * 128 : direction * 128 + 125, :125] = whole
    return np.concatenate(halves_of(table), axis=1)


def side_constant():
    rows = np.full((1, 768), -1.0, np.float32)
    for side in range(6):
        for coord in range(3):
            at = side * 128 + coord * 25
            rows[0, at : at + 25] = [coord * 128 + node for node in side_nodes(side)]
    return rows


def quadrant_tables():
    for quadrant in range(4):
        first = UPPER if quadrant & 2 else LOWER
        second = UPPER if quadrant & 1 else LOWER
        yield np.kron(first, second)


def tangent_constant():
    slopes = [np.kron(SLOPE, EYE), np.kron(EYE, SLOPE)]
    parts = []
    for placed in [np.eye(25)] + list(quadrant_tables()):
        table = np.zeros((128, 256))
        for which, slope in enumerate(slopes):
            whole = 0.5 * (slope @ placed)
            for spot, coord in enumerate((0, 1, 2, 0, 1)):
                at = which * 128 + spot * 25
                table[coord * 25 : coord * 25 + 25, at : at + 25] = whole.T
        parts += halves_of(table)
    return np.concatenate(parts, axis=0)


def back_constant():
    parts = []
    for placed in quadrant_tables():
        table = np.zeros((128, 128))
        for coord in range(3):
            at = coord * 25
            table[at : at + 25, at : at + 25] = placed
        parts += halves_of(table)
    return np.concatenate(parts, axis=0)


def dot(left, right):
    return lax.dot_general(left, right, (((1,), (0,)), ((), ())), preferred_element_type=F32)


def dot_nt(left, right):
    return lax.dot_general(left, right, (((1,), (1,)), ((), ())), preferred_element_type=F32)


def split(value):
    high = value.astype(BF16)
    return high, (value - high.astype(F32)).astype(BF16)


def triple(value, axis=1):
    high, low = split(value)
    return jnp.concatenate([high, low, high], axis=axis)


def tripled(constant, size, axis=0):
    parts = []
    for at in range(0, constant.shape[axis], 2 * size):
        high = lax.slice_in_dim(constant, at, at + size, axis=axis)
        low = lax.slice_in_dim(constant, at + size, at + 2 * size, axis=axis)
        parts += [high, high, low]
    return jnp.concatenate(parts, axis=axis)


def side_matrix(rows):
    return ones_where(iota((384, rows.shape[1]), 0) == rows)


def iota(shape, axis):
    return lax.broadcasted_iota(jnp.int32, shape, axis).astype(F32)


def ones_where(condition):
    return jnp.where(condition, 1.0, 0.0).astype(BF16)


def pick(blocks, key):
    chosen = blocks[0]
    for number in range(1, len(blocks)):
        chosen = jnp.where(key == float(number), blocks[number], chosen)
    return chosen


def lane_blocks(value, count):
    return [value[:, 128 * b : 128 * b + 128] for b in range(count)]


def positions(owner):
    records = owner.shape[1]
    column = columns_of(owner)[:, 0:1]
    same = (column == owner) & (iota((records, records), 0) < iota((records, records), 1))
    return owner * 2.0 + jnp.sum(jnp.where(same, 1.0, 0.0), axis=0, keepdims=True)


def columns_of(rows):
    count = rows.shape[1]
    eye = ones_where(iota((count, count), 0) == iota((count, count), 1))
    padded = jnp.broadcast_to(rows, (8, count)) if rows.shape[0] == 1 else rows
    return dot_nt(eye, padded.astype(BF16))


def child_table(pool, child_k):
    table = dot(triple(pool), tripled(child_k, 128))
    stacked = [
        jnp.concatenate(
            [
                table[c * POOL : (c + 1) * POOL, o * 128 : o * 128 + 128]
                for c in range(3)
            ],
            axis=1,
        )
        for o in range(8)
    ]
    high, low = split(jnp.concatenate(stacked, axis=0))
    return jnp.concatenate([high, low], axis=0)


def row_picker(key, size):
    hot = ones_where(key == iota((key.shape[0], size), 1))
    return jnp.concatenate([hot, hot], axis=1)


def messages(table, side_k, slots, position, ints):
    faces = dot(table, side_k).astype(BF16)
    hot = ones_where(iota((slots, position.shape[1]), 0) == position)
    carried = dot_nt(hot, ints.astype(BF16))
    filled = carried[:, VALID : VALID + 1]
    key = carried[:, OCT : OCT + 1] * float(POOL) + carried[:, PROW : PROW + 1]
    picker = row_picker(jnp.where(filled > 0.5, key, -1.0), 8 * POOL)
    sides = dot(picker, faces)
    face = pick(lane_blocks(sides, 6), carried[:, FSIDE : FSIDE + 1])
    return jnp.where(iota(face.shape, 1) < 75.0, face, carried)


def determinants(table, slope_k, keys):
    children = dot(row_picker(keys, 8 * POOL), table)
    slope_k = tripled(slope_k, 128, 1)
    grads = [dot_nt(slope_k, triple(block)) for block in lane_blocks(children, 3)]
    g = [[grads[c][128 * d : 128 * d + 128] for c in range(3)] for d in range(3)]
    first = g[0][0] * (g[1][1] * g[2][2] - g[2][1] * g[1][2])
    second = g[1][0] * (g[0][1] * g[2][2] - g[2][1] * g[0][2])
    third = g[2][0] * (g[0][1] * g[1][2] - g[1][1] * g[0][2])
    return first - second + third


def coarse_faces(coarse, side_k):
    high, low = split(coarse.T)
    return jnp.concatenate([dot(high, side_k), dot(low, side_k)], axis=1).astype(BF16)


def mortar(message, faces, tangent_k):
    slots = message.shape[0]
    elements = faces.shape[0]
    filled = message[:, VALID : VALID + 1] > 0.5
    elem = jnp.where(filled, message[:, ELEM : ELEM + 1], -1.0)
    side, quad = message[:, SIDE : SIDE + 1], message[:, QUAD : QUAD + 1]
    hot = ones_where(elem == iota((slots, elements), 1))
    blocks = lane_blocks(dot(hot, faces), 12)
    high, low = pick(blocks[:6], side), pick(blocks[6:], side)
    parts = [triple(message)]
    for number in range(4):
        mine = quad == float(number)
        this_high = jnp.where(mine, high, 0.0).astype(BF16)
        this_low = jnp.where(mine, low, 0.0).astype(BF16)
        parts += [this_high, this_low, this_high]
    tangents = dot(jnp.concatenate(parts, axis=1), tripled(tangent_k, 128))
    t1, t2 = tangents[:, :128], tangents[:, 128:]
    ahead = lambda value, count: pltpu.roll(value, 128 - 25 * count, 1)
    return ahead(t1, 1) * ahead(t2, 2) - ahead(t1, 2) * ahead(t2, 1)


def partial_sums(normal, message, back_k, elements):
    slots = message.shape[0]
    filled = message[:, VALID : VALID + 1] > 0.5
    side, quad = message[:, SIDE : SIDE + 1], message[:, QUAD : QUAD + 1]
    key = side * float(elements) + message[:, ELEM : ELEM + 1]
    key = jnp.where(filled, key, -1.0)
    parts = []
    for number in range(4):
        parts.append(triple(jnp.where(quad == float(number), normal, 0.0)))
    back = dot(jnp.concatenate(parts, axis=1), tripled(back_k, 128))
    high, low = split(back.T)
    hot = ones_where(key == iota((slots, 6 * elements), 1))
    both = dot(jnp.concatenate([high, low], axis=0), hot)
    return both[:128] + both[128:]


def face_rows(returned, position):
    hot = ones_where(iota((returned.shape[0], position.shape[1]), 0) == position)
    high, low = split(returned.T)
    both = dot(jnp.concatenate([high, low], axis=0), hot)
    return both[:128] + both[128:]


def fill_pool(pool, parents, previous):
    pool[...] = jnp.zeros(pool.shape, F32)
    for c in range(3):
        own = parents[c]
        pool[c * POOL : c * POOL + 32, 0:125] = own - own[:, MIDDLE : MIDDLE + 1]
        last = previous[c : c + 1, 0:125]
        pool[c * POOL + 32 : c * POOL + 33, 0:125] = last - last[:, MIDDLE : MIDDLE + 1]


def fill_coarse(scratch, coarse):
    for c in range(3):
        scratch[c * 128 + 120 : c * 128 + 128, :] = jnp.zeros((8, coarse.shape[2]), F32)
        whole = coarse[c]
        scratch[c * 128 : c * 128 + 125, :] = whole - whole[MIDDLE : MIDDLE + 1]


def fill_ints(scratch, parent, octant, elem, side, c_elem, c_side, quad):
    scratch[...] = jnp.zeros(scratch.shape, F32)
    elements = parent.shape[1]
    parent = jnp.where(parent < 0.0, 32.0, parent)
    both = jnp.concatenate([parent, octant, jnp.zeros((6, elements), F32)], axis=0)
    hot = ones_where(iota((elements, elem.shape[1]), 0) == elem)
    chosen = dot(both.astype(BF16), hot)
    scratch[VALID : VALID + 1, :] = jnp.ones_like(elem)
    scratch[ELEM : ELEM + 1, :] = c_elem
    scratch[SIDE : SIDE + 1, :] = c_side
    scratch[QUAD : QUAD + 1, :] = quad
    scratch[FSIDE : FSIDE + 1, :] = side
    scratch[PROW : PROW + 1, :] = chosen[0:1]
    scratch[OCT : OCT + 1, :] = chosen[1:2]
    turned = columns_of(both)
    return turned[:, 1:2] * float(POOL) + turned[:, 0:1]


def fine_kernel(slots, parents, previous, parent, octant, elem, side, owner, c_elem, c_side, quad,
                child_k, side_k, slope_k, message_out, jac_out, pool, ints):
    rows = [r[...].astype(F32) for r in (parent, octant, elem, side, c_elem, c_side, quad)]
    fill_pool(pool, parents, previous)
    keys = fill_ints(ints, *rows)
    table = child_table(pool[...], child_k[...])
    position = positions(owner[...].astype(F32))
    message_out[...] = messages(table, side_matrix(side_k[...]), slots, position, ints[...])
    jac_out[...] = determinants(table, slope_k[...], keys)[0:125]


def mortar_kernel(message_in, coarse, side_k, tangent_k, back_k, normal_out, partial_out, scratch):
    elements = coarse.shape[2]
    fill_coarse(scratch, coarse)
    faces = coarse_faces(scratch[...], side_matrix(side_k[...]))
    message = message_in[...]
    normal = mortar(message, faces, tangent_k[...])
    normal_out[...] = normal
    sums = partial_sums(normal, message, back_k[...], elements)
    write_partials(partial_out, sums, elements)


def write_partials(partial_out, sums, elements):
    for c in range(3):
        for s in range(6):
            partial_out[c, s * 25 : s * 25 + 25, :] = sums[
                c * 25 : c * 25 + 25, s * elements : (s + 1) * elements
            ]


def final_kernel(returned, owner, normals_out):
    rows = face_rows(returned[...], positions(owner[...].astype(F32)))
    for c in range(3):
        normals_out[c] = rows[c * 25 : c * 25 + 25]


def call(kernel, shapes, scratch, *args):
    return pl.pallas_call(
        kernel,
        out_shape=shapes,
        scratch_shapes=scratch,
        compiler_params=pltpu.CompilerParams(vmem_limit_bytes=48 << 20),
    )(*args)


def shards(parents, coarse, parent, octant, elem, side, owner, c_elem, c_side, quad):
    axes = ("leaf", "dom")
    ranks = lax.axis_size(axes)
    slots = 2 * ranks
    records, elements = elem.shape[0], parent.shape[0]
    row = lambda value: value.reshape(1, -1)
    previous = lax.ppermute(
        parents[:, :, -1], axes, [(source, source + 1) for source in range(ranks - 1)]
    )
    side_k = side_constant()
    message, jac = call(
        functools.partial(fine_kernel, slots),
        (
            jax.ShapeDtypeStruct((slots, 128), F32),
            jax.ShapeDtypeStruct((125, elements), F32),
        ),
        [pltpu.VMEM((3 * POOL, 128), F32), pltpu.VMEM((128, records), F32)],
        parents.transpose(0, 2, 1), previous, row(parent), row(octant), row(elem), row(side),
        row(owner), row(c_elem), row(c_side), row(quad),
        jnp.asarray(child_constant()), jnp.asarray(side_k), jnp.asarray(slope_constant()),
    )
    arrived = lax.all_to_all(message.reshape(ranks, 2, 128), axes, 0, 0, tiled=True)
    normal, partials = call(
        mortar_kernel,
        (
            jax.ShapeDtypeStruct((slots, 128), F32),
            jax.ShapeDtypeStruct((3, 150, coarse.shape[2]), F32),
        ),
        [pltpu.VMEM((384, coarse.shape[2]), F32)],
        arrived.reshape(slots, 128), coarse,
        jnp.asarray(side_k), jnp.asarray(tangent_constant()),
        jnp.asarray(back_constant()),
    )
    returned = lax.all_to_all(normal.reshape(ranks, 2, 128), axes, 0, 0, tiled=True)
    normals = call(
        final_kernel,
        jax.ShapeDtypeStruct((3, 25, records), F32),
        [],
        returned.reshape(slots, 128), row(owner),
    )
    return jac, normals, partials


def solution(mesh):
    whole = P(None, None, ("leaf", "dom"))
    line = P(("leaf", "dom"))
    return jax.shard_map(
        shards,
        mesh=mesh,
        in_specs=(whole, whole, line, line, line, line, P(("leaf", "dom"), None), line, line, line),
        out_specs=(P(None, ("leaf", "dom")), whole, whole),
        check_vma=False,
    )
```

```python
import functools
import math

import jax
import jax.numpy as jnp
import ml_dtypes
import numpy as np
from jax import lax
from jax.experimental import pallas as pl
from jax.experimental.pallas import tpu as pltpu
from jax.sharding import PartitionSpec as P

F32 = jnp.float32
BF16 = jnp.bfloat16
POOL = 40
MIDDLE = 62
VALID, ELEM, SIDE, QUAD, FSIDE, PROW, OCT = 75, 76, 77, 78, 80, 81, 82


def lobatto_nodes():
    return np.array([-1.0, -math.sqrt(3.0 / 7.0), 0.0, math.sqrt(3.0 / 7.0), 1.0])


def lagrange_table(targets):
    points = lobatto_nodes()
    table = np.ones((targets.shape[0], 5))
    for column in range(5):
        for others in range(5):
            if others != column:
                table[:, column] *= (targets - points[others]) / (points[column] - points[others])
    return table


def derivative_table():
    points = lobatto_nodes()
    table = np.zeros((5, 5))
    for target in range(5):
        for column in range(5):
            total = 0.0
            for others in range(5):
                if others != column:
                    term = 1.0 / (points[column] - points[others])
                    for remain in range(5):
                        if remain != column and remain != others:
                            term *= (points[target] - points[remain]) / (
                                points[column] - points[remain]
                            )
                    total += term
            table[target, column] = total
    return table


def f32_table(table):
    return table.astype(np.float32).astype(np.float64)


LOWER = f32_table(lagrange_table((lobatto_nodes() - 1.0) / 2.0))
UPPER = f32_table(lagrange_table((lobatto_nodes() + 1.0) / 2.0))
SLOPE = f32_table(derivative_table())
EYE = np.eye(5)


def halves_of(table):
    high = table.astype(np.float32).astype(ml_dtypes.bfloat16)
    low = (table - high.astype(np.float64)).astype(np.float32).astype(ml_dtypes.bfloat16)
    return high, low


def side_nodes(side):
    direction, level = side // 2, side % 2 * 4
    fixed = (25, 5, 1)[direction]
    first = 5 if direction == 0 else 25
    second = 5 if direction == 2 else 1
    return [level * fixed + a * first + b * second for a in range(5) for b in range(5)]


def child_constant():
    table = np.zeros((128, 8 * 128))
    for octant in range(8):
        picks = [UPPER if octant & bit else LOWER for bit in (4, 2, 1)]
        whole = np.kron(np.kron(picks[0], picks[1]), picks[2])
        table[:125, octant * 128 : octant * 128 + 125] = whole.T
    return np.concatenate(halves_of(table), axis=0)


def slope_constant():
    table = np.zeros((384, 128))
    for direction in range(3):
        picks = [SLOPE if axis == direction else EYE for axis in range(3)]
        whole = np.kron(np.kron(picks[0], picks[1]), picks[2])
        table[direction * 128 : direction * 128 + 125, :125] = whole
    return np.concatenate(halves_of(table), axis=1)


def side_constant():
    rows = np.full((1, 768), -1.0, np.float32)
    for side in range(6):
        for coord in range(3):
            at = side * 128 + coord * 25
            rows[0, at : at + 25] = [coord * 128 + node for node in side_nodes(side)]
    return rows


def quadrant_tables():
    for quadrant in range(4):
        first = UPPER if quadrant & 2 else LOWER
        second = UPPER if quadrant & 1 else LOWER
        yield np.kron(first, second)


def tangent_constant():
    slopes = [np.kron(SLOPE, EYE), np.kron(EYE, SLOPE)]
    parts = []
    for placed in [np.eye(25)] + list(quadrant_tables()):
        table = np.zeros((128, 256))
        for which, slope in enumerate(slopes):
            whole = 0.5 * (slope @ placed)
            for spot, coord in enumerate((0, 1, 2, 0, 1)):
                at = which * 128 + spot * 25
                table[coord * 25 : coord * 25 + 25, at : at + 25] = whole.T
        parts += halves_of(table)
    return np.concatenate(parts, axis=0)


def back_constant():
    parts = []
    for placed in quadrant_tables():
        table = np.zeros((128, 128))
        for coord in range(3):
            at = coord * 25
            table[at : at + 25, at : at + 25] = placed
        parts += halves_of(table)
    return np.concatenate(parts, axis=0)


def dot(left, right):
    return lax.dot_general(left, right, (((1,), (0,)), ((), ())), preferred_element_type=F32)


def dot_nt(left, right):
    return lax.dot_general(left, right, (((1,), (1,)), ((), ())), preferred_element_type=F32)


def split(value):
    high = value.astype(BF16)
    return high, (value - high.astype(F32)).astype(BF16)


def triple(value, axis=1):
    high, low = split(value)
    return jnp.concatenate([high, low, high], axis=axis)


def tripled(constant, size, axis=0):
    parts = []
    for at in range(0, constant.shape[axis], 2 * size):
        high = lax.slice_in_dim(constant, at, at + size, axis=axis)
        low = lax.slice_in_dim(constant, at + size, at + 2 * size, axis=axis)
        parts += [high, high, low]
    return jnp.concatenate(parts, axis=axis)


def side_matrix(rows):
    return ones_where(iota((384, rows.shape[1]), 0) == rows)


def iota(shape, axis):
    return lax.broadcasted_iota(jnp.int32, shape, axis).astype(F32)


def ones_where(condition):
    return jnp.where(condition, 1.0, 0.0).astype(BF16)


def pick(blocks, key):
    chosen = blocks[0]
    for number in range(1, len(blocks)):
        chosen = jnp.where(key == float(number), blocks[number], chosen)
    return chosen


def lane_blocks(value, count):
    return [value[:, 128 * b : 128 * b + 128] for b in range(count)]


def positions(owner):
    records = owner.shape[1]
    column = columns_of(owner)[:, 0:1]
    same = (column == owner) & (iota((records, records), 0) < iota((records, records), 1))
    return owner * 2.0 + jnp.sum(jnp.where(same, 1.0, 0.0), axis=0, keepdims=True)


def columns_of(rows):
    count = rows.shape[1]
    eye = ones_where(iota((count, count), 0) == iota((count, count), 1))
    padded = jnp.broadcast_to(rows, (8, count)) if rows.shape[0] == 1 else rows
    return dot_nt(eye, padded.astype(BF16))


def child_table(pool, child_k):
    table = dot(triple(pool), tripled(child_k, 128))
    stacked = [
        jnp.concatenate(
            [
                table[c * POOL : (c + 1) * POOL, o * 128 : o * 128 + 128]
                for c in range(3)
            ],
            axis=1,
        )
        for o in range(8)
    ]
    high, low = split(jnp.concatenate(stacked, axis=0))
    return jnp.concatenate([high, low], axis=0)


def row_picker(key, size):
    hot = ones_where(key == iota((key.shape[0], size), 1))
    return jnp.concatenate([hot, hot], axis=1)


def messages(table, side_k, slots, position, ints):
    faces = dot(table, side_k).astype(BF16)
    hot = ones_where(iota((slots, position.shape[1]), 0) == position)
    carried = dot_nt(hot, ints.astype(BF16))
    filled = carried[:, VALID : VALID + 1]
    key = carried[:, OCT : OCT + 1] * float(POOL) + carried[:, PROW : PROW + 1]
    picker = row_picker(jnp.where(filled > 0.5, key, -1.0), 8 * POOL)
    sides = dot(picker, faces)
    face = pick(lane_blocks(sides, 6), carried[:, FSIDE : FSIDE + 1])
    return jnp.where(iota(face.shape, 1) < 75.0, face, carried)


def determinants(table, slope_k, keys):
    children = dot(row_picker(keys, 8 * POOL), table)
    slope_k = tripled(slope_k, 128, 1)
    grads = [dot_nt(slope_k, triple(block)) for block in lane_blocks(children, 3)]
    g = [[grads[c][128 * d : 128 * d + 128] for c in range(3)] for d in range(3)]
    first = g[0][0] * (g[1][1] * g[2][2] - g[2][1] * g[1][2])
    second = g[1][0] * (g[0][1] * g[2][2] - g[2][1] * g[0][2])
    third = g[2][0] * (g[0][1] * g[1][2] - g[1][1] * g[0][2])
    return first - second + third


def coarse_faces(coarse, side_k):
    high, low = split(coarse.T)
    return jnp.concatenate([dot(high, side_k), dot(low, side_k)], axis=1).astype(BF16)


def mortar(message, faces, tangent_k):
    slots = message.shape[0]
    elements = faces.shape[0]
    filled = message[:, VALID : VALID + 1] > 0.5
    elem = jnp.where(filled, message[:, ELEM : ELEM + 1], -1.0)
    side, quad = message[:, SIDE : SIDE + 1], message[:, QUAD : QUAD + 1]
    hot = ones_where(elem == iota((slots, elements), 1))
    blocks = lane_blocks(dot(hot, faces), 12)
    high, low = pick(blocks[:6], side), pick(blocks[6:], side)
    parts = [triple(message)]
    for number in range(4):
        mine = quad == float(number)
        this_high = jnp.where(mine, high, 0.0).astype(BF16)
        this_low = jnp.where(mine, low, 0.0).astype(BF16)
        parts += [this_high, this_low, this_high]
    tangents = dot(jnp.concatenate(parts, axis=1), tripled(tangent_k, 128))
    t1, t2 = tangents[:, :128], tangents[:, 128:]
    ahead = lambda value, count: pltpu.roll(value, 128 - 25 * count, 1)
    return ahead(t1, 1) * ahead(t2, 2) - ahead(t1, 2) * ahead(t2, 1)


def partial_sums(normal, message, back_k, elements):
    slots = message.shape[0]
    filled = message[:, VALID : VALID + 1] > 0.5
    side, quad = message[:, SIDE : SIDE + 1], message[:, QUAD : QUAD + 1]
    key = side * float(elements) + message[:, ELEM : ELEM + 1]
    key = jnp.where(filled, key, -1.0)
    parts = []
    for number in range(4):
        parts.append(triple(jnp.where(quad == float(number), normal, 0.0)))
    back = dot(jnp.concatenate(parts, axis=1), tripled(back_k, 128))
    high, low = split(back.T)
    hot = ones_where(key == iota((slots, 6 * elements), 1))
    both = dot(jnp.concatenate([high, low], axis=0), hot)
    return both[:128] + both[128:]


def face_rows(returned, position):
    hot = ones_where(iota((returned.shape[0], position.shape[1]), 0) == position)
    high, low = split(returned.T)
    both = dot(jnp.concatenate([high, low], axis=0), hot)
    return both[:128] + both[128:]


def fill_pool(pool, parents, previous):
    pool[...] = jnp.zeros(pool.shape, F32)
    for c in range(3):
        own = parents[c]
        pool[c * POOL : c * POOL + 32, 0:125] = own - own[:, MIDDLE : MIDDLE + 1]
        last = previous[c : c + 1, 0:125]
        pool[c * POOL + 32 : c * POOL + 33, 0:125] = last - last[:, MIDDLE : MIDDLE + 1]


def fill_coarse(scratch, coarse):
    for c in range(3):
        scratch[c * 128 + 120 : c * 128 + 128, :] = jnp.zeros((8, coarse.shape[2]), F32)
        whole = coarse[c]
        scratch[c * 128 : c * 128 + 125, :] = whole - whole[MIDDLE : MIDDLE + 1]


def fill_ints(scratch, parent, octant, elem, side, c_elem, c_side, quad):
    scratch[...] = jnp.zeros(scratch.shape, F32)
    elements = parent.shape[1]
    parent = jnp.where(parent < 0.0, 32.0, parent)
    both = jnp.concatenate([parent, octant, jnp.zeros((6, elements), F32)], axis=0)
    hot = ones_where(iota((elements, elem.shape[1]), 0) == elem)
    chosen = dot(both.astype(BF16), hot)
    scratch[VALID : VALID + 1, :] = jnp.ones_like(elem)
    scratch[ELEM : ELEM + 1, :] = c_elem
    scratch[SIDE : SIDE + 1, :] = c_side
    scratch[QUAD : QUAD + 1, :] = quad
    scratch[FSIDE : FSIDE + 1, :] = side
    scratch[PROW : PROW + 1, :] = chosen[0:1]
    scratch[OCT : OCT + 1, :] = chosen[1:2]
    turned = columns_of(both)
    return turned[:, 1:2] * float(POOL) + turned[:, 0:1]


def write_partials(partial_out, sums, elements):
    for c in range(3):
        for s in range(6):
            partial_out[c, s * 25 : s * 25 + 25, :] = sums[
                c * 25 : c * 25 + 25, s * elements : (s + 1) * elements
            ]


def everyone_else(leaves, doms, leaf, dom, act):
    for ahead in range(leaves):
        there = lax.rem(leaf + ahead, leaves)

        def body(other, carry):
            act(there, other)
            return carry

        lax.fori_loop(dom + 1, doms, body, 0)
        lax.fori_loop(0, dom, body, 0)
        if ahead:
            act(there, dom)


def kernel(leaves, doms, parents, previous, parent, octant, elem, side, owner, c_elem, c_side,
           quad, coarse, child_k, side_k, slope_k, tangent_k, back_k,
           jac_out, normals_out, partial_out,
           pool, ints, scratch, fine_send, fine_here, normal_send, normal_here, sems):
    leaf, dom = lax.axis_index("leaf"), lax.axis_index("dom")
    me = leaf * doms + dom
    ranks = leaves * doms
    slots = 2 * ranks
    elements = coarse.shape[2]
    barrier = pltpu.get_barrier_semaphore()

    def greet(l, d):
        pl.semaphore_signal(
            barrier, inc=1, device_id=(l, d), device_id_type=pl.DeviceIdType.MESH
        )

    everyone_else(leaves, doms, leaf, dom, greet)

    def exchange(source, target, send_sem, recv_sem):
        def send(l, d):
            pltpu.make_async_remote_copy(
                src_ref=source.at[l * doms + d],
                dst_ref=target.at[me],
                send_sem=send_sem,
                recv_sem=recv_sem,
                device_id=(l, d),
                device_id_type=pl.DeviceIdType.MESH,
            ).start()

        everyone_else(leaves, doms, leaf, dom, send)
        target[pl.ds(me, 1)] = source[pl.ds(me, 1)]

    def wait_all(ref, sem):
        most = ref.at[pl.ds(0, ranks - 1)]
        pltpu.make_async_copy(most, most, sem).wait()

    rows = [r[...].astype(F32) for r in (parent, octant, elem, side, c_elem, c_side, quad)]
    fill_pool(pool, parents, previous)
    keys = fill_ints(ints, *rows)
    table = child_table(pool[...], child_k[...])
    position = positions(owner[...].astype(F32))
    sides = side_matrix(side_k[...])
    message = messages(table, sides, slots, position, ints[...])
    fine_send[...] = message.reshape(fine_send.shape)
    pl.semaphore_wait(barrier, ranks - 1)
    exchange(fine_send, fine_here, sems.at[0], sems.at[1])

    jac_out[...] = determinants(table, slope_k[...], keys)[0:125]
    fill_coarse(scratch, coarse)
    faces = coarse_faces(scratch[...], sides)

    wait_all(fine_here, sems.at[1])
    message = fine_here[...].reshape(slots, 128)
    normal = mortar(message, faces, tangent_k[...])
    normal_send[...] = normal.reshape(normal_send.shape)
    exchange(normal_send, normal_here, sems.at[2], sems.at[3])

    write_partials(partial_out, partial_sums(normal, message, back_k[...], elements), elements)

    wait_all(normal_here, sems.at[3])
    returned = face_rows(normal_here[...].reshape(slots, 128), position)
    for c in range(3):
        normals_out[c] = returned[c * 25 : c * 25 + 25]
    wait_all(fine_send, sems.at[0])
    wait_all(normal_send, sems.at[2])


def shards(parents, coarse, parent, octant, elem, side, owner, c_elem, c_side, quad):
    axes = ("leaf", "dom")
    leaves, doms = lax.axis_size("leaf"), lax.axis_size("dom")
    ranks = leaves * doms
    records, elements = elem.shape[0], parent.shape[0]
    row = lambda value: value.reshape(1, -1)
    previous = lax.ppermute(
        parents[:, :, -1], axes, [(source, source + 1) for source in range(ranks - 1)]
    )
    buffer = pltpu.VMEM((ranks, 2, 128), F32)
    return pl.pallas_call(
        functools.partial(kernel, leaves, doms),
        out_shape=(
            jax.ShapeDtypeStruct((125, elements), F32),
            jax.ShapeDtypeStruct((3, 25, records), F32),
            jax.ShapeDtypeStruct((3, 150, coarse.shape[2]), F32),
        ),
        scratch_shapes=[
            pltpu.VMEM((3 * POOL, 128), F32),
            pltpu.VMEM((128, records), F32),
            pltpu.VMEM((384, coarse.shape[2]), F32),
            buffer, buffer, buffer, buffer,
            pltpu.SemaphoreType.DMA((4,)),
        ],
        compiler_params=pltpu.CompilerParams(
            collective_id=0, has_side_effects=True, vmem_limit_bytes=40 << 20
        ),
    )(
        parents.transpose(0, 2, 1), previous, row(parent), row(octant), row(elem), row(side),
        row(owner), row(c_elem), row(c_side), row(quad), coarse,
        jnp.asarray(child_constant()), jnp.asarray(side_constant()),
        jnp.asarray(slope_constant()), jnp.asarray(tangent_constant()),
        jnp.asarray(back_constant()),
    )


def solution(mesh):
    whole = P(None, None, ("leaf", "dom"))
    line = P(("leaf", "dom"))
    return jax.shard_map(
        shards,
        mesh=mesh,
        in_specs=(whole, whole, line, line, line, line, P(("leaf", "dom"), None), line, line, line),
        out_specs=(P(None, ("leaf", "dom")), whole, whole),
        check_vma=False,
    )
```

```python
import functools
import math

import jax
import jax.numpy as jnp
import ml_dtypes
import numpy as np
from jax import lax
from jax.experimental import pallas as pl
from jax.experimental.pallas import tpu as pltpu
from jax.sharding import PartitionSpec as P

F32 = jnp.float32
BF16 = jnp.bfloat16
POOL = 32
MIDDLE = 62
GROUP = 1
VALID, ELEM, SIDE, QUAD, FSIDE, PROW, OCT = 75, 76, 77, 78, 80, 81, 82


def lobatto_nodes():
    return np.array([-1.0, -math.sqrt(3.0 / 7.0), 0.0, math.sqrt(3.0 / 7.0), 1.0])


def lagrange_table(targets):
    points = lobatto_nodes()
    table = np.ones((targets.shape[0], 5))
    for column in range(5):
        for others in range(5):
            if others != column:
                table[:, column] *= (targets - points[others]) / (points[column] - points[others])
    return table


def derivative_table():
    points = lobatto_nodes()
    table = np.zeros((5, 5))
    for target in range(5):
        for column in range(5):
            total = 0.0
            for others in range(5):
                if others != column:
                    term = 1.0 / (points[column] - points[others])
                    for remain in range(5):
                        if remain != column and remain != others:
                            term *= (points[target] - points[remain]) / (
                                points[column] - points[remain]
                            )
                    total += term
            table[target, column] = total
    return table


def f32_table(table):
    return table.astype(np.float32).astype(np.float64)


LOWER = f32_table(lagrange_table((lobatto_nodes() - 1.0) / 2.0))
UPPER = f32_table(lagrange_table((lobatto_nodes() + 1.0) / 2.0))
SLOPE = f32_table(derivative_table())
EYE = np.eye(5)


def halves_of(table):
    high = table.astype(np.float32).astype(ml_dtypes.bfloat16)
    low = (table - high.astype(np.float64)).astype(np.float32).astype(ml_dtypes.bfloat16)
    return high, low


def side_nodes(side):
    direction, level = side // 2, side % 2 * 4
    fixed = (25, 5, 1)[direction]
    first = 5 if direction == 0 else 25
    second = 5 if direction == 2 else 1
    return [level * fixed + a * first + b * second for a in range(5) for b in range(5)]


def child_constant():
    table = np.zeros((128, 8 * 128))
    for octant in range(8):
        picks = [UPPER if octant & bit else LOWER for bit in (4, 2, 1)]
        whole = np.kron(np.kron(picks[0], picks[1]), picks[2])
        table[:125, octant * 128 : octant * 128 + 125] = whole.T
    return np.concatenate(halves_of(table), axis=0)


def slope_constant():
    table = np.zeros((384, 128))
    for direction in range(3):
        picks = [SLOPE if axis == direction else EYE for axis in range(3)]
        whole = np.kron(np.kron(picks[0], picks[1]), picks[2])
        table[direction * 128 : direction * 128 + 125, :125] = whole
    return np.concatenate(halves_of(table), axis=1)


def side_constant():
    rows = np.full((1, 768), -1.0, np.float32)
    for side in range(6):
        for coord in range(3):
            at = side * 128 + coord * 25
            rows[0, at : at + 25] = [coord * 128 + node for node in side_nodes(side)]
    return rows


def quadrant_tables():
    for quadrant in range(4):
        first = UPPER if quadrant & 2 else LOWER
        second = UPPER if quadrant & 1 else LOWER
        yield np.kron(first, second)


def tangent_constant():
    slopes = [np.kron(SLOPE, EYE), np.kron(EYE, SLOPE)]
    parts = []
    for placed in [np.eye(25)] + list(quadrant_tables()):
        table = np.zeros((128, 256))
        for which, slope in enumerate(slopes):
            whole = 0.5 * (slope @ placed)
            for spot, coord in enumerate((0, 1, 2, 0, 1)):
                at = which * 128 + spot * 25
                table[coord * 25 : coord * 25 + 25, at : at + 25] = whole.T
        parts += halves_of(table)
    return np.concatenate(parts, axis=0)


def back_constant():
    parts = []
    for placed in quadrant_tables():
        table = np.zeros((128, 128))
        for coord in range(3):
            at = coord * 25
            table[at : at + 25, at : at + 25] = placed
        parts += halves_of(table)
    return np.concatenate(parts, axis=0)


def dot(left, right):
    return lax.dot_general(left, right, (((1,), (0,)), ((), ())), preferred_element_type=F32)


def dot_nt(left, right):
    return lax.dot_general(left, right, (((1,), (1,)), ((), ())), preferred_element_type=F32)


def split(value):
    high = value.astype(BF16)
    return high, (value - high.astype(F32)).astype(BF16)


def triple(value, axis=1):
    high, low = split(value)
    return jnp.concatenate([high, low, high], axis=axis)


def tripled(constant, size, axis=0):
    parts = []
    for at in range(0, constant.shape[axis], 2 * size):
        high = lax.slice_in_dim(constant, at, at + size, axis=axis)
        low = lax.slice_in_dim(constant, at + size, at + 2 * size, axis=axis)
        parts += [high, high, low]
    return jnp.concatenate(parts, axis=axis)


def side_matrix(rows):
    return ones_where(iota((384, rows.shape[1]), 0) == rows)


def iota(shape, axis):
    return lax.broadcasted_iota(jnp.int32, shape, axis).astype(F32)


def ones_where(condition):
    return jnp.where(condition, 1.0, 0.0).astype(BF16)


def pick(blocks, key):
    chosen = blocks[0]
    for number in range(1, len(blocks)):
        chosen = jnp.where(key == float(number), blocks[number], chosen)
    return chosen


def lane_blocks(value, count):
    return [value[:, 128 * b : 128 * b + 128] for b in range(count)]


def positions(owner):
    records = owner.shape[1]
    column = columns_of(owner)[:, 0:1]
    same = (column == owner) & (iota((records, records), 0) < iota((records, records), 1))
    return owner * 2.0 + jnp.sum(jnp.where(same, 1.0, 0.0), axis=0, keepdims=True)


def columns_of(rows):
    count = rows.shape[1]
    eye = ones_where(iota((count, count), 0) == iota((count, count), 1))
    padded = jnp.broadcast_to(rows, (8, count)) if rows.shape[0] == 1 else rows
    return dot_nt(eye, padded.astype(BF16))


def child_table(pool, child_k):
    table = dot(triple(pool), tripled(child_k, 128))
    count = pool.shape[0] // 3
    stacked = [
        jnp.concatenate(
            [table[c * count : (c + 1) * count, o * 128 : o * 128 + 128] for c in range(3)], axis=1
        )
        for o in range(8)
    ]
    high, low = split(jnp.concatenate(stacked, axis=0))
    return jnp.concatenate([high.astype(F32), low.astype(F32)], axis=0).astype(BF16)


def row_picker(key, size):
    places = iota((key.shape[0], 2 * size), 1)
    places = jnp.where(places >= float(size), places - float(size), places)
    return ones_where(key == places)


def keys_of(parent, octant, filled):
    own = jnp.where(filled & (parent >= 0.0), octant * float(POOL) + parent, -1.0)
    halo = jnp.where(filled & (parent < 0.0), octant, -1.0)
    return own, halo


def messages(table, sides, slots, position, ints):
    faces = dot(table, sides).astype(BF16)
    hot = ones_where(iota((slots, position.shape[1]), 0) == position)
    carried = dot_nt(hot, ints.astype(BF16))
    filled = carried[:, VALID : VALID + 1] > 0.5
    side = carried[:, FSIDE : FSIDE + 1]
    own, halo = keys_of(carried[:, PROW : PROW + 1], carried[:, OCT : OCT + 1], filled)
    face = pick(lane_blocks(dot(row_picker(own, 8 * POOL), faces), 6), side)
    base = jnp.where(iota(face.shape, 1) < 75.0, face, carried)
    return base, jnp.where(halo >= 0.0, side * 8.0 + halo, -1.0)


def halo_messages(halo_table, sides, keys):
    faces = dot(halo_table, sides)
    rows = [block[8 * h : 8 * h + 8] for h in range(2) for block in lane_blocks(faces, 6)]
    return dot(row_picker(keys, 48), jnp.concatenate(rows, axis=0).astype(BF16))


def determinants(table, halo_table, slope_k, own, halo):
    children = dot(row_picker(own, 8 * POOL), table) + dot(row_picker(halo, 8), halo_table)
    slope_k = tripled(slope_k, 128, 1)
    grads = [dot_nt(slope_k, triple(block)) for block in lane_blocks(children, 3)]
    g = [[grads[c][128 * d : 128 * d + 128] for c in range(3)] for d in range(3)]
    first = g[0][0] * (g[1][1] * g[2][2] - g[2][1] * g[1][2])
    second = g[1][0] * (g[0][1] * g[2][2] - g[2][1] * g[0][2])
    third = g[2][0] * (g[0][1] * g[1][2] - g[1][1] * g[0][2])
    return first - second + third


def coarse_faces(coarse, side_k):
    high, low = split(coarse.T)
    return jnp.concatenate([dot(high, side_k), dot(low, side_k)], axis=1).astype(BF16)


def mortar(message, faces, tangent_k):
    slots = message.shape[0]
    elements = faces.shape[0]
    filled = message[:, VALID : VALID + 1] > 0.5
    elem = jnp.where(filled, message[:, ELEM : ELEM + 1], -1.0)
    side, quad = message[:, SIDE : SIDE + 1], message[:, QUAD : QUAD + 1]
    hot = ones_where(elem == iota((slots, elements), 1))
    blocks = lane_blocks(dot(hot, faces), 12)
    high, low = pick(blocks[:6], side), pick(blocks[6:], side)
    parts = [triple(message)]
    for number in range(4):
        mine = quad == float(number)
        this_high = jnp.where(mine, high, 0.0).astype(BF16)
        this_low = jnp.where(mine, low, 0.0).astype(BF16)
        parts += [this_high, this_low, this_high]
    tangents = dot(jnp.concatenate(parts, axis=1), tripled(tangent_k, 128))
    t1, t2 = tangents[:, :128], tangents[:, 128:]
    ahead = lambda value, count: pltpu.roll(value, 128 - 25 * count, 1)
    return ahead(t1, 1) * ahead(t2, 2) - ahead(t1, 2) * ahead(t2, 1)


def partial_sums(normal, message, back_k, elements):
    slots = message.shape[0]
    filled = message[:, VALID : VALID + 1] > 0.5
    side, quad = message[:, SIDE : SIDE + 1], message[:, QUAD : QUAD + 1]
    key = side * float(elements) + message[:, ELEM : ELEM + 1]
    key = jnp.where(filled, key, -1.0)
    parts = []
    for number in range(4):
        parts.append(triple(jnp.where(quad == float(number), normal, 0.0)))
    back = dot(jnp.concatenate(parts, axis=1), tripled(back_k, 128))
    high, low = split(back.T)
    hot = ones_where(key == iota((slots, 6 * elements), 1))
    both = dot(jnp.concatenate([high, low], axis=0), hot)
    return both[:128] + both[128:]


def face_rows(returned, position):
    hot = ones_where(iota((returned.shape[0], position.shape[1]), 0) == position)
    high, low = split(returned.T)
    both = dot(jnp.concatenate([high, low], axis=0), hot)
    return both[:128] + both[128:]


def fill_pool(pool, last, parents):
    pool[...] = jnp.zeros(pool.shape, F32)
    last[...] = jnp.zeros(last.shape, F32)
    for c in range(3):
        own = parents[c]
        own = own - own[:, MIDDLE : MIDDLE + 1]
        pool[c * POOL : (c + 1) * POOL, 0:125] = own
        last[c : c + 1, 0:125] = own[POOL - 1 :]


def fill_coarse(scratch, coarse):
    for c in range(3):
        scratch[c * 128 + 120 : c * 128 + 128, :] = jnp.zeros((8, coarse.shape[2]), F32)
        whole = coarse[c]
        scratch[c * 128 : c * 128 + 125, :] = whole - whole[MIDDLE : MIDDLE + 1]


def fill_ints(scratch, parent, octant, elem, side, c_elem, c_side, quad):
    scratch[...] = jnp.zeros(scratch.shape, F32)
    elements = parent.shape[1]
    both = jnp.concatenate([parent, octant, jnp.zeros((6, elements), F32)], axis=0)
    hot = ones_where(iota((elements, elem.shape[1]), 0) == elem)
    chosen = dot(both.astype(BF16), hot)
    scratch[VALID : VALID + 1, :] = jnp.ones_like(elem)
    scratch[ELEM : ELEM + 1, :] = c_elem
    scratch[SIDE : SIDE + 1, :] = c_side
    scratch[QUAD : QUAD + 1, :] = quad
    scratch[FSIDE : FSIDE + 1, :] = side
    scratch[PROW : PROW + 1, :] = chosen[0:1]
    scratch[OCT : OCT + 1, :] = chosen[1:2]
    turned = columns_of(both)
    return keys_of(turned[:, 0:1], turned[:, 1:2], turned[:, 1:2] >= 0.0)


def write_partials(partial_out, sums, elements):
    for c in range(3):
        for s in range(6):
            partial_out[c, s * 25 : s * 25 + 25, :] = sums[
                c * 25 : c * 25 + 25, s * elements : (s + 1) * elements
            ]


INPUTS = ("parent", "octant", "elem", "owner", "side", "c_elem", "c_side", "quad", "parents",
          "child_k", "side_k", "coarse", "slope_k", "tangent_k", "back_k")


def kernel(leaves, doms, groups, *refs):
    count = len(INPUTS)
    sources = refs[:count]
    jac_out, normals_out, partial_out = refs[count : count + 3]
    copies = refs[count + 3 : 2 * count + 3]
    (pool, last, halo_in, ints, scratch, fine_send, fine_here, normal_send, normal_here,
     in_sems, halo_sems, send_sems, fine_sems, normal_sems) = refs[2 * count + 3 :]
    leaf, dom = lax.axis_index("leaf"), lax.axis_index("dom")
    ranks = leaves * doms
    me = leaf * doms + dom
    slots = 2 * ranks
    mesh_id = pl.DeviceIdType.MESH

    loads = {
        name: pltpu.make_async_copy(sources[at], copies[at], in_sems.at[at])
        for at, name in enumerate(INPUTS)
    }
    for name in INPUTS:
        loads[name].start()

    def load(name):
        loads[name].wait()
        return copies[INPUTS.index(name)]

    def others(ahead, act):
        there = lax.rem(leaf + ahead, leaves)

        def body(other, carry):
            act(there, other)
            return carry

        lax.fori_loop(dom + 1, doms, body, 0)
        lax.fori_loop(0, dom, body, 0)
        if ahead:
            act(there, dom)

    barrier = pltpu.get_barrier_semaphore()

    def greet(l, d):
        pl.semaphore_signal(barrier, inc=1, device_id=(l, d), device_id_type=mesh_id)

    for ahead in range(leaves):
        others(ahead, greet)

    def send_all(ahead, source, target, send_sem, recv_sem):
        def send(l, d):
            pltpu.make_async_remote_copy(
                src_ref=source.at[l * doms + d],
                dst_ref=target.at[me],
                send_sem=send_sem,
                recv_sem=recv_sem,
                device_id=(l, d),
                device_id_type=mesh_id,
            ).start()

        others(ahead, send)

    def wait_rows(ref, rows, sem):
        most = ref.at[pl.ds(0, rows)]
        pltpu.make_async_copy(most, most, sem).wait()

    def wait_leaf(ref, back, sems):
        wait_rows(ref, doms if back else doms - 1, sems.at[back])

    names = ("parent", "octant", "elem", "side", "c_elem", "c_side", "quad")
    own_keys, halo_keys = fill_ints(ints, *[load(name)[...].astype(F32) for name in names])
    position = positions(load("owner")[...].astype(F32))
    fill_pool(pool, last, load("parents"))
    child_k = load("child_k")[...]
    table = child_table(pool[...], child_k)
    sides = side_matrix(load("side_k")[...])
    message, message_keys = messages(table, sides, slots, position, ints[...])

    pl.semaphore_wait(barrier, ranks - 1)
    after = lax.rem(me + 1, ranks)
    halo = pltpu.make_async_remote_copy(
        src_ref=last,
        dst_ref=halo_in,
        send_sem=halo_sems.at[0],
        recv_sem=halo_sems.at[1],
        device_id=(after // doms, lax.rem(after, doms)),
        device_id_type=mesh_id,
    )
    halo.start()
    scratch_ref = load("coarse")
    elements = scratch_ref.shape[2]
    fill_coarse(scratch, scratch_ref)
    faces = coarse_faces(scratch[...], sides)
    halo.wait()
    halo_table = child_table(jnp.concatenate([halo_in[c : c + 1] for c in range(3)], axis=0), child_k)
    message = message + halo_messages(halo_table, sides, message_keys)
    fine_send[...] = message.reshape(fine_send.shape)
    for ahead in range(leaves):
        send_all(ahead, fine_send, fine_here, send_sems.at[0], fine_sems.at[ahead])
    fine_here[pl.ds(me, 1)] = fine_send[pl.ds(me, 1)]

    slope_k = load("slope_k")[...]
    jac_out[...] = determinants(table, halo_table, slope_k, own_keys, halo_keys)[0:125]
    tangent_k = load("tangent_k")[...]
    back_k = load("back_k")[...]

    for group in groups:
        starts = [lax.rem(leaf + leaves - back, leaves) * doms for back in group]
        for back in group:
            wait_leaf(fine_here, back, fine_sems)
        rows = [fine_here[pl.ds(start, doms)].reshape(2 * doms, 128) for start in starts]
        normal = mortar(jnp.concatenate(rows, axis=0), faces, tangent_k)
        for number, (back, start) in enumerate(zip(group, starts)):
            mine = normal[number * 2 * doms : (number + 1) * 2 * doms]
            normal_send[pl.ds(start, doms)] = mine.reshape(doms, 2, 128)
        for back in group:
            send_all(
                (leaves - back) % leaves, normal_send, normal_here, send_sems.at[1],
                normal_sems.at[(leaves - back) % leaves],
            )
    normal_here[pl.ds(me, 1)] = normal_send[pl.ds(me, 1)]

    normal = normal_send[...].reshape(slots, 128)
    message = fine_here[...].reshape(slots, 128)
    write_partials(partial_out, partial_sums(normal, message, back_k, elements), elements)

    for back in range(leaves):
        wait_leaf(normal_here, back, normal_sems)
    returned = face_rows(normal_here[...].reshape(slots, 128), position)
    for c in range(3):
        normals_out[c] = returned[c * 25 : c * 25 + 25]
    wait_rows(fine_send, ranks - 1, send_sems.at[0])
    wait_rows(normal_send, ranks - 1, send_sems.at[1])


def store_kernel(*refs):
    count = (len(refs) - 1) // 2
    copies = [
        pltpu.make_async_copy(refs[at], refs[count + at], refs[-1].at[at]) for at in range(count)
    ]
    for copy in copies:
        copy.start()
    for copy in copies:
        copy.wait()


def shards(parents, coarse, parent, octant, elem, side, owner, c_elem, c_side, quad):
    leaves, doms = lax.axis_size("leaf"), lax.axis_size("dom")
    ranks = leaves * doms
    records, elements = elem.shape[0], parent.shape[0]
    row = lambda value: value.reshape(1, -1)
    given = dict(
        parent=row(parent), octant=row(octant), elem=row(elem), side=row(side), owner=row(owner),
        c_elem=row(c_elem), c_side=row(c_side), quad=row(quad),
        parents=parents.transpose(0, 2, 1), coarse=coarse,
        child_k=jnp.asarray(child_constant()), side_k=jnp.asarray(side_constant()),
        slope_k=jnp.asarray(slope_constant()), tangent_k=jnp.asarray(tangent_constant()),
        back_k=jnp.asarray(back_constant()),
    )
    args = [given[name] for name in INPUTS]
    buffer = pltpu.VMEM((ranks, 2, 128), F32)
    groups = [list(range(leaves))[at : at + GROUP] for at in range(0, leaves, GROUP)]
    shapes = (
        jax.ShapeDtypeStruct((125, elements), F32),
        jax.ShapeDtypeStruct((3, 25, records), F32),
        jax.ShapeDtypeStruct((3, 150, coarse.shape[2]), F32),
    )
    results = pl.pallas_call(
        functools.partial(kernel, leaves, doms, groups),
        out_shape=shapes,
        in_specs=[pl.BlockSpec(memory_space=pltpu.HBM)] * len(args),
        out_specs=[pl.BlockSpec(memory_space=pltpu.VMEM)] * 3,
        scratch_shapes=[pltpu.VMEM(arg.shape, arg.dtype) for arg in args] + [
            pltpu.VMEM((3 * POOL, 128), F32),
            pltpu.VMEM((8, 128), F32),
            pltpu.VMEM((8, 128), F32),
            pltpu.VMEM((128, records), F32),
            pltpu.VMEM((384, coarse.shape[2]), F32),
            buffer, buffer, buffer, buffer,
            pltpu.SemaphoreType.DMA((len(args),)),
            pltpu.SemaphoreType.DMA((2,)),
            pltpu.SemaphoreType.DMA((2,)),
            pltpu.SemaphoreType.DMA((leaves,)),
            pltpu.SemaphoreType.DMA((leaves,)),
        ],
        compiler_params=pltpu.CompilerParams(
            collective_id=0, has_side_effects=True
        ),
    )(*args)
    return pl.pallas_call(
        store_kernel,
        out_shape=shapes,
        in_specs=[pl.BlockSpec(memory_space=pltpu.VMEM)] * 3,
        out_specs=[pl.BlockSpec(memory_space=pltpu.HBM)] * 3,
        scratch_shapes=[pltpu.SemaphoreType.DMA((3,))],
    )(*results)


def solution(mesh):
    whole = P(None, None, ("leaf", "dom"))
    line = P(("leaf", "dom"))
    return jax.shard_map(
        shards,
        mesh=mesh,
        in_specs=(whole, whole, line, line, line, line, P(("leaf", "dom"), None), line, line, line),
        out_specs=(P(None, ("leaf", "dom")), whole, whole),
        check_vma=False,
    )
```

```python
import functools
import math

import jax
import jax.numpy as jnp
import ml_dtypes
import numpy as np
from jax import lax
from jax.experimental import pallas as pl
from jax.experimental.pallas import tpu as pltpu
from jax.sharding import PartitionSpec as P

F32 = jnp.float32
BF16 = jnp.bfloat16
POOL = 32
MIDDLE = 62
GROUP = 1
VALID, ELEM, SIDE, QUAD, FSIDE, PROW, OCT = 75, 76, 77, 78, 80, 81, 82


def lobatto_nodes():
    return np.array([-1.0, -math.sqrt(3.0 / 7.0), 0.0, math.sqrt(3.0 / 7.0), 1.0])


def lagrange_table(targets):
    points = lobatto_nodes()
    table = np.ones((targets.shape[0], 5))
    for column in range(5):
        for others in range(5):
            if others != column:
                table[:, column] *= (targets - points[others]) / (points[column] - points[others])
    return table


def derivative_table():
    points = lobatto_nodes()
    table = np.zeros((5, 5))
    for target in range(5):
        for column in range(5):
            total = 0.0
            for others in range(5):
                if others != column:
                    term = 1.0 / (points[column] - points[others])
                    for remain in range(5):
                        if remain != column and remain != others:
                            term *= (points[target] - points[remain]) / (
                                points[column] - points[remain]
                            )
                    total += term
            table[target, column] = total
    return table


def f32_table(table):
    return table.astype(np.float32).astype(np.float64)


LOWER = f32_table(lagrange_table((lobatto_nodes() - 1.0) / 2.0))
UPPER = f32_table(lagrange_table((lobatto_nodes() + 1.0) / 2.0))
SLOPE = f32_table(derivative_table())
EYE = np.eye(5)


def halves_of(table):
    high = table.astype(np.float32).astype(ml_dtypes.bfloat16)
    low = (table - high.astype(np.float64)).astype(np.float32).astype(ml_dtypes.bfloat16)
    return high, low


def side_nodes(side):
    direction, level = side // 2, side % 2 * 4
    fixed = (25, 5, 1)[direction]
    first = 5 if direction == 0 else 25
    second = 5 if direction == 2 else 1
    return [level * fixed + a * first + b * second for a in range(5) for b in range(5)]


def child_constant():
    table = np.zeros((128, 8 * 128))
    for octant in range(8):
        picks = [UPPER if octant & bit else LOWER for bit in (4, 2, 1)]
        whole = np.kron(np.kron(picks[0], picks[1]), picks[2])
        table[:125, octant * 128 : octant * 128 + 125] = whole.T
    return np.concatenate(halves_of(table), axis=0)


def slope_constant():
    table = np.zeros((384, 128))
    for direction in range(3):
        picks = [SLOPE if axis == direction else EYE for axis in range(3)]
        whole = np.kron(np.kron(picks[0], picks[1]), picks[2])
        table[direction * 128 : direction * 128 + 125, :125] = whole
    return np.concatenate(halves_of(table), axis=1)


def side_constant():
    rows = np.full((1, 768), -1.0, np.float32)
    for side in range(6):
        for coord in range(3):
            at = side * 128 + coord * 25
            rows[0, at : at + 25] = [coord * 128 + node for node in side_nodes(side)]
    return rows


def quadrant_tables():
    for quadrant in range(4):
        first = UPPER if quadrant & 2 else LOWER
        second = UPPER if quadrant & 1 else LOWER
        yield np.kron(first, second)


def tangent_constant():
    slopes = [np.kron(SLOPE, EYE), np.kron(EYE, SLOPE)]
    parts = []
    for placed in [np.eye(25)] + list(quadrant_tables()):
        table = np.zeros((128, 256))
        for which, slope in enumerate(slopes):
            whole = 0.5 * (slope @ placed)
            for spot, coord in enumerate((0, 1, 2, 0, 1)):
                at = which * 128 + spot * 25
                table[coord * 25 : coord * 25 + 25, at : at + 25] = whole.T
        parts += halves_of(table)
    return np.concatenate(parts, axis=0)


def back_constant():
    parts = []
    for placed in quadrant_tables():
        table = np.zeros((128, 128))
        for coord in range(3):
            at = coord * 25
            table[at : at + 25, at : at + 25] = placed
        parts += halves_of(table)
    return np.concatenate(parts, axis=0)


def dot(left, right):
    return lax.dot_general(left, right, (((1,), (0,)), ((), ())), preferred_element_type=F32)


def dot_nt(left, right):
    return lax.dot_general(left, right, (((1,), (1,)), ((), ())), preferred_element_type=F32)


def split(value):
    high = value.astype(BF16)
    return high, (value - high.astype(F32)).astype(BF16)


def triple(value, axis=1):
    high, low = split(value)
    return jnp.concatenate([high, low, high], axis=axis)


def tripled(constant, size, axis=0):
    parts = []
    for at in range(0, constant.shape[axis], 2 * size):
        high = lax.slice_in_dim(constant, at, at + size, axis=axis)
        low = lax.slice_in_dim(constant, at + size, at + 2 * size, axis=axis)
        parts += [high, high, low]
    return jnp.concatenate(parts, axis=axis)


def side_matrix(rows):
    return ones_where(iota((384, rows.shape[1]), 0) == rows)


def iota(shape, axis):
    return lax.broadcasted_iota(jnp.int32, shape, axis).astype(F32)


def ones_where(condition):
    return jnp.where(condition, 1.0, 0.0).astype(BF16)


def pick(blocks, key):
    chosen = blocks[0]
    for number in range(1, len(blocks)):
        chosen = jnp.where(key == float(number), blocks[number], chosen)
    return chosen


def lane_blocks(value, count):
    return [value[:, 128 * b : 128 * b + 128] for b in range(count)]


def positions(owner):
    records = owner.shape[1]
    column = columns_of(owner)[:, 0:1]
    same = (column == owner) & (iota((records, records), 0) < iota((records, records), 1))
    return owner * 2.0 + jnp.sum(jnp.where(same, 1.0, 0.0), axis=0, keepdims=True)


def columns_of(rows):
    count = rows.shape[1]
    eye = ones_where(iota((count, count), 0) == iota((count, count), 1))
    padded = jnp.broadcast_to(rows, (8, count)) if rows.shape[0] == 1 else rows
    return dot_nt(eye, padded.astype(BF16))


def child_table(pool, child_k):
    table = dot(triple(pool), tripled(child_k, 128))
    count = pool.shape[0] // 3
    stacked = [
        jnp.concatenate(
            [table[c * count : (c + 1) * count, o * 128 : o * 128 + 128] for c in range(3)], axis=1
        )
        for o in range(8)
    ]
    high, low = split(jnp.concatenate(stacked, axis=0))
    return jnp.concatenate([high.astype(F32), low.astype(F32)], axis=0).astype(BF16)


def row_picker(key, size):
    places = iota((key.shape[0], 2 * size), 1)
    places = jnp.where(places >= float(size), places - float(size), places)
    return ones_where(key == places)


def keys_of(parent, octant, filled):
    own = jnp.where(filled & (parent >= 0.0), octant * float(POOL) + parent, -1.0)
    halo = jnp.where(filled & (parent < 0.0), octant, -1.0)
    return own, halo


def messages(table, sides, slots, position, ints):
    faces = dot(table, sides).astype(BF16)
    hot = ones_where(iota((slots, position.shape[1]), 0) == position)
    carried = dot_nt(hot, ints.astype(BF16))
    filled = carried[:, VALID : VALID + 1] > 0.5
    side = carried[:, FSIDE : FSIDE + 1]
    own, halo = keys_of(carried[:, PROW : PROW + 1], carried[:, OCT : OCT + 1], filled)
    face = pick(lane_blocks(dot(row_picker(own, 8 * POOL), faces), 6), side)
    base = jnp.where(iota(face.shape, 1) < 75.0, face, carried)
    return base, jnp.where(halo >= 0.0, side * 8.0 + halo, -1.0)


def halo_messages(halo_table, sides, keys):
    faces = dot(halo_table, sides)
    rows = [block[8 * h : 8 * h + 8] for h in range(2) for block in lane_blocks(faces, 6)]
    return dot(row_picker(keys, 48), jnp.concatenate(rows, axis=0).astype(BF16))


def determinants(table, halo_table, slope_k, own, halo):
    children = dot(row_picker(own, 8 * POOL), table) + dot(row_picker(halo, 8), halo_table)
    slope_k = tripled(slope_k, 128, 1)
    grads = [dot_nt(slope_k, triple(block)) for block in lane_blocks(children, 3)]
    g = [[grads[c][128 * d : 128 * d + 128] for c in range(3)] for d in range(3)]
    first = g[0][0] * (g[1][1] * g[2][2] - g[2][1] * g[1][2])
    second = g[1][0] * (g[0][1] * g[2][2] - g[2][1] * g[0][2])
    third = g[2][0] * (g[0][1] * g[1][2] - g[1][1] * g[0][2])
    return first - second + third


def coarse_faces(coarse, side_k):
    high, low = split(coarse.T)
    return jnp.concatenate([dot(high, side_k), dot(low, side_k)], axis=1).astype(BF16)


def mortar(message, faces, tangent_k):
    slots = message.shape[0]
    elements = faces.shape[0]
    filled = message[:, VALID : VALID + 1] > 0.5
    elem = jnp.where(filled, message[:, ELEM : ELEM + 1], -1.0)
    side, quad = message[:, SIDE : SIDE + 1], message[:, QUAD : QUAD + 1]
    hot = ones_where(elem == iota((slots, elements), 1))
    blocks = lane_blocks(dot(hot, faces), 12)
    high, low = pick(blocks[:6], side), pick(blocks[6:], side)
    parts = [triple(message)]
    for number in range(4):
        mine = quad == float(number)
        this_high = jnp.where(mine, high, 0.0).astype(BF16)
        this_low = jnp.where(mine, low, 0.0).astype(BF16)
        parts += [this_high, this_low, this_high]
    tangents = dot(jnp.concatenate(parts, axis=1), tripled(tangent_k, 128))
    t1, t2 = tangents[:, :128], tangents[:, 128:]
    ahead = lambda value, count: pltpu.roll(value, 128 - 25 * count, 1)
    return ahead(t1, 1) * ahead(t2, 2) - ahead(t1, 2) * ahead(t2, 1)


def partial_sums(normal, message, back_k, elements):
    slots = message.shape[0]
    filled = message[:, VALID : VALID + 1] > 0.5
    side, quad = message[:, SIDE : SIDE + 1], message[:, QUAD : QUAD + 1]
    key = side * float(elements) + message[:, ELEM : ELEM + 1]
    key = jnp.where(filled, key, -1.0)
    parts = []
    for number in range(4):
        parts.append(triple(jnp.where(quad == float(number), normal, 0.0)))
    back = dot(jnp.concatenate(parts, axis=1), tripled(back_k, 128))
    high, low = split(back.T)
    hot = ones_where(key == iota((slots, 6 * elements), 1))
    both = dot(jnp.concatenate([high, low], axis=0), hot)
    return both[:128] + both[128:]


def face_rows(returned, position):
    hot = ones_where(iota((returned.shape[0], position.shape[1]), 0) == position)
    high, low = split(returned.T)
    both = dot(jnp.concatenate([high, low], axis=0), hot)
    return both[:128] + both[128:]


def fill_pool(pool, last, parents):
    pool[...] = jnp.zeros(pool.shape, F32)
    last[...] = jnp.zeros(last.shape, F32)
    for c in range(3):
        own = parents[c]
        own = own - own[:, MIDDLE : MIDDLE + 1]
        pool[c * POOL : (c + 1) * POOL, 0:125] = own
        last[c : c + 1, 0:125] = own[POOL - 1 :]


def fill_coarse(scratch, coarse):
    for c in range(3):
        scratch[c * 128 + 120 : c * 128 + 128, :] = jnp.zeros((8, coarse.shape[2]), F32)
        whole = coarse[c]
        scratch[c * 128 : c * 128 + 125, :] = whole - whole[MIDDLE : MIDDLE + 1]


def fill_ints(scratch, parent, octant, elem, side, c_elem, c_side, quad):
    scratch[...] = jnp.zeros(scratch.shape, F32)
    elements = parent.shape[1]
    both = jnp.concatenate([parent, octant, jnp.zeros((6, elements), F32)], axis=0)
    hot = ones_where(iota((elements, elem.shape[1]), 0) == elem)
    chosen = dot(both.astype(BF16), hot)
    scratch[VALID : VALID + 1, :] = jnp.ones_like(elem)
    scratch[ELEM : ELEM + 1, :] = c_elem
    scratch[SIDE : SIDE + 1, :] = c_side
    scratch[QUAD : QUAD + 1, :] = quad
    scratch[FSIDE : FSIDE + 1, :] = side
    scratch[PROW : PROW + 1, :] = chosen[0:1]
    scratch[OCT : OCT + 1, :] = chosen[1:2]
    turned = columns_of(both)
    return keys_of(turned[:, 0:1], turned[:, 1:2], turned[:, 1:2] >= 0.0)


def write_partials(partial_out, sums, elements):
    for c in range(3):
        for s in range(6):
            partial_out[c, s * 25 : s * 25 + 25, :] = sums[
                c * 25 : c * 25 + 25, s * elements : (s + 1) * elements
            ]


INPUTS = ("parent", "octant", "elem", "owner", "side", "c_elem", "c_side", "quad", "parents",
          "child_k", "side_k", "coarse", "slope_k", "tangent_k", "back_k")


def kernel(leaves, doms, groups, *refs):
    count = len(INPUTS)
    sources = refs[:count]
    jac_out, normals_out, partial_out = refs[count : count + 3]
    copies = refs[count + 3 : 2 * count + 3]
    (pool, last, halo_in, ints, scratch, fine_send, fine_here, normal_send, normal_here,
     in_sems, halo_sems, send_sems, fine_sems, normal_sems) = refs[2 * count + 3 :]
    leaf, dom = lax.axis_index("leaf"), lax.axis_index("dom")
    ranks = leaves * doms
    me = leaf * doms + dom
    slots = 2 * ranks
    mesh_id = pl.DeviceIdType.MESH

    loads = {
        name: pltpu.make_async_copy(sources[at], copies[at], in_sems.at[at])
        for at, name in enumerate(INPUTS)
    }
    for name in INPUTS:
        loads[name].start()

    def load(name):
        loads[name].wait()
        return copies[INPUTS.index(name)]

    xs = max(doms // 16, 1)
    zs = doms // (2 * xs)
    at_x, at_z, core = dom // (2 * zs), lax.rem(dom // 2, zs), lax.rem(dom, 2)
    z_steps = sorted(range(zs), key=lambda step: -min(step, zs - step))
    by_z = [(step, lax.rem(at_z + step, zs) * 2) for step in z_steps]
    by_core = [(1, 1 - core), (0, core)]

    def others(ahead, act):
        there = lax.rem(leaf + ahead, leaves)

        def plane(step_x, skip):
            base = lax.rem(at_x + step_x, xs) * (2 * zs)
            for step_z, z_part in by_z:
                for step_core, core_part in by_core:
                    if not (skip and step_z == 0 and step_core == 0):
                        act(there, base + z_part + core_part)

        def body(number, carry):
            plane(number + xs // 2, False)
            return carry

        if ahead:
            lax.fori_loop(0, xs, body, 0)
        else:
            for number in range(xs):
                step_x = (number + xs // 2) % xs
                plane(step_x, step_x == 0)

    far_first = sorted(range(leaves), key=lambda step: -min(step, leaves - step))

    barrier = pltpu.get_barrier_semaphore()

    def greet(l, d):
        pl.semaphore_signal(barrier, inc=1, device_id=(l, d), device_id_type=mesh_id)

    for ahead in far_first:
        others(ahead, greet)

    def send_all(ahead, source, target, send_sem, recv_sem):
        def send(l, d):
            pltpu.make_async_remote_copy(
                src_ref=source.at[l * doms + d],
                dst_ref=target.at[me],
                send_sem=send_sem,
                recv_sem=recv_sem,
                device_id=(l, d),
                device_id_type=mesh_id,
            ).start()

        others(ahead, send)

    def wait_rows(ref, rows, sem):
        most = ref.at[pl.ds(0, rows)]
        pltpu.make_async_copy(most, most, sem).wait()

    def wait_leaf(ref, back, sems):
        wait_rows(ref, doms if back else doms - 1, sems.at[back])

    names = ("parent", "octant", "elem", "side", "c_elem", "c_side", "quad")
    own_keys, halo_keys = fill_ints(ints, *[load(name)[...].astype(F32) for name in names])
    position = positions(load("owner")[...].astype(F32))
    fill_pool(pool, last, load("parents"))
    child_k = load("child_k")[...]
    table = child_table(pool[...], child_k)
    sides = side_matrix(load("side_k")[...])
    message, message_keys = messages(table, sides, slots, position, ints[...])

    pl.semaphore_wait(barrier, ranks - 1)
    after = lax.rem(me + 1, ranks)
    halo = pltpu.make_async_remote_copy(
        src_ref=last,
        dst_ref=halo_in,
        send_sem=halo_sems.at[0],
        recv_sem=halo_sems.at[1],
        device_id=(after // doms, lax.rem(after, doms)),
        device_id_type=mesh_id,
    )
    halo.start()
    scratch_ref = load("coarse")
    elements = scratch_ref.shape[2]
    fill_coarse(scratch, scratch_ref)
    faces = coarse_faces(scratch[...], sides)
    halo.wait()
    halo_table = child_table(jnp.concatenate([halo_in[c : c + 1] for c in range(3)], axis=0), child_k)
    message = message + halo_messages(halo_table, sides, message_keys)
    fine_send[...] = message.reshape(fine_send.shape)
    for ahead in far_first:
        send_all(ahead, fine_send, fine_here, send_sems.at[0], fine_sems.at[ahead])
    fine_here[pl.ds(me, 1)] = fine_send[pl.ds(me, 1)]

    slope_k = load("slope_k")[...]
    jac_out[...] = determinants(table, halo_table, slope_k, own_keys, halo_keys)[0:125]
    tangent_k = load("tangent_k")[...]
    back_k = load("back_k")[...]

    for group in groups:
        starts = [lax.rem(leaf + leaves - back, leaves) * doms for back in group]
        for back in group:
            wait_leaf(fine_here, back, fine_sems)
        rows = [fine_here[pl.ds(start, doms)].reshape(2 * doms, 128) for start in starts]
        normal = mortar(jnp.concatenate(rows, axis=0), faces, tangent_k)
        for number, (back, start) in enumerate(zip(group, starts)):
            mine = normal[number * 2 * doms : (number + 1) * 2 * doms]
            normal_send[pl.ds(start, doms)] = mine.reshape(doms, 2, 128)
        for back in group:
            send_all(
                (leaves - back) % leaves, normal_send, normal_here, send_sems.at[1],
                normal_sems.at[(leaves - back) % leaves],
            )
    normal_here[pl.ds(me, 1)] = normal_send[pl.ds(me, 1)]

    normal = normal_send[...].reshape(slots, 128)
    message = fine_here[...].reshape(slots, 128)
    write_partials(partial_out, partial_sums(normal, message, back_k, elements), elements)

    for back in range(leaves):
        wait_leaf(normal_here, back, normal_sems)
    returned = face_rows(normal_here[...].reshape(slots, 128), position)
    for c in range(3):
        normals_out[c] = returned[c * 25 : c * 25 + 25]
    wait_rows(fine_send, ranks - 1, send_sems.at[0])
    wait_rows(normal_send, ranks - 1, send_sems.at[1])


def shards(parents, coarse, parent, octant, elem, side, owner, c_elem, c_side, quad):
    leaves, doms = lax.axis_size("leaf"), lax.axis_size("dom")
    ranks = leaves * doms
    records, elements = elem.shape[0], parent.shape[0]
    row = lambda value: value.reshape(1, -1)
    given = dict(
        parent=row(parent), octant=row(octant), elem=row(elem), side=row(side), owner=row(owner),
        c_elem=row(c_elem), c_side=row(c_side), quad=row(quad),
        parents=parents.transpose(0, 2, 1), coarse=coarse,
        child_k=jnp.asarray(child_constant()), side_k=jnp.asarray(side_constant()),
        slope_k=jnp.asarray(slope_constant()), tangent_k=jnp.asarray(tangent_constant()),
        back_k=jnp.asarray(back_constant()),
    )
    args = [pltpu.with_memory_space_constraint(given[name], pltpu.HBM) for name in INPUTS]
    buffer = pltpu.VMEM((ranks, 2, 128), F32)
    far_first = sorted(range(leaves), key=lambda step: -min(step, leaves - step))
    groups = [far_first[at : at + GROUP] for at in range(0, leaves, GROUP)]
    shapes = (
        jax.ShapeDtypeStruct((125, elements), F32),
        jax.ShapeDtypeStruct((3, 25, records), F32),
        jax.ShapeDtypeStruct((3, 150, coarse.shape[2]), F32),
    )
    return pl.pallas_call(
        functools.partial(kernel, leaves, doms, groups),
        out_shape=shapes,
        in_specs=[pl.BlockSpec(memory_space=pltpu.HBM)] * len(args),
        out_specs=[pl.BlockSpec(memory_space=pltpu.VMEM)] * 3,
        scratch_shapes=[pltpu.VMEM(arg.shape, arg.dtype) for arg in args] + [
            pltpu.VMEM((3 * POOL, 128), F32),
            pltpu.VMEM((8, 128), F32),
            pltpu.VMEM((8, 128), F32),
            pltpu.VMEM((128, records), F32),
            pltpu.VMEM((384, coarse.shape[2]), F32),
            buffer, buffer, buffer, buffer,
            pltpu.SemaphoreType.DMA((len(args),)),
            pltpu.SemaphoreType.DMA((2,)),
            pltpu.SemaphoreType.DMA((2,)),
            pltpu.SemaphoreType.DMA((leaves,)),
            pltpu.SemaphoreType.DMA((leaves,)),
        ],
        compiler_params=pltpu.CompilerParams(
            collective_id=0, has_side_effects=True, vmem_limit_bytes=40 << 20
        ),
    )(*args)


def solution(mesh):
    whole = P(None, None, ("leaf", "dom"))
    line = P(("leaf", "dom"))
    return jax.shard_map(
        shards,
        mesh=mesh,
        in_specs=(whole, whole, line, line, line, line, P(("leaf", "dom"), None), line, line, line),
        out_specs=(P(None, ("leaf", "dom")), whole, whole),
        check_vma=False,
    )
```

```python
import functools
import math

import jax
import jax.numpy as jnp
import ml_dtypes
import numpy as np
from jax import lax
from jax.experimental import pallas as pl
from jax.experimental.pallas import tpu as pltpu
from jax.sharding import PartitionSpec as P

F32 = jnp.float32
BF16 = jnp.bfloat16
POOL = 32
MIDDLE = 62
GROUP = 1
VALID, ELEM, SIDE, QUAD, FSIDE, PROW, OCT = range(7)
SECOND = 64


def lobatto_nodes():
    return np.array([-1.0, -math.sqrt(3.0 / 7.0), 0.0, math.sqrt(3.0 / 7.0), 1.0])


def lagrange_table(targets):
    points = lobatto_nodes()
    table = np.ones((targets.shape[0], 5))
    for column in range(5):
        for others in range(5):
            if others != column:
                table[:, column] *= (targets - points[others]) / (points[column] - points[others])
    return table


def derivative_table():
    points = lobatto_nodes()
    table = np.zeros((5, 5))
    for target in range(5):
        for column in range(5):
            total = 0.0
            for others in range(5):
                if others != column:
                    term = 1.0 / (points[column] - points[others])
                    for remain in range(5):
                        if remain != column and remain != others:
                            term *= (points[target] - points[remain]) / (
                                points[column] - points[remain]
                            )
                    total += term
            table[target, column] = total
    return table


def f32_table(table):
    return table.astype(np.float32).astype(np.float64)


LOWER = f32_table(lagrange_table((lobatto_nodes() - 1.0) / 2.0))
UPPER = f32_table(lagrange_table((lobatto_nodes() + 1.0) / 2.0))
SLOPE = f32_table(derivative_table())
EYE = np.eye(5)


def halves_of(table):
    high = table.astype(np.float32).astype(ml_dtypes.bfloat16)
    low = (table - high.astype(np.float64)).astype(np.float32).astype(ml_dtypes.bfloat16)
    return high, low


def side_nodes(side):
    direction, level = side // 2, side % 2 * 4
    fixed = (25, 5, 1)[direction]
    first = 5 if direction == 0 else 25
    second = 5 if direction == 2 else 1
    return [level * fixed + a * first + b * second for a in range(5) for b in range(5)]


def child_constant():
    table = np.zeros((128, 8 * 128))
    for octant in range(8):
        picks = [UPPER if octant & bit else LOWER for bit in (4, 2, 1)]
        whole = np.kron(np.kron(picks[0], picks[1]), picks[2])
        table[:125, octant * 128 : octant * 128 + 125] = whole.T
    return np.concatenate(halves_of(table), axis=0)


def slope_constant():
    table = np.zeros((384, 128))
    for direction in range(3):
        picks = [SLOPE if axis == direction else EYE for axis in range(3)]
        whole = np.kron(np.kron(picks[0], picks[1]), picks[2])
        table[direction * 128 : direction * 128 + 125, :125] = whole
    return np.concatenate(halves_of(table), axis=1)


def side_constant():
    rows = np.full((1, 768), -1.0, np.float32)
    for side in range(6):
        for coord in range(3):
            at = side * 128 + coord * 25
            rows[0, at : at + 25] = [coord * 128 + node for node in side_nodes(side)]
    return rows


def quadrant_tables():
    for quadrant in range(4):
        first = UPPER if quadrant & 2 else LOWER
        second = UPPER if quadrant & 1 else LOWER
        yield np.kron(first, second)


def tangent_constant():
    slopes = [np.kron(SLOPE, EYE), np.kron(EYE, SLOPE)]
    parts = []
    for placed in [np.eye(25)] + list(quadrant_tables()):
        table = np.zeros((128, 256))
        for which, slope in enumerate(slopes):
            whole = 0.5 * (slope @ placed)
            for spot, coord in enumerate((0, 1, 2, 0, 1)):
                at = which * 128 + spot * 25
                table[coord * 25 : coord * 25 + 25, at : at + 25] = whole.T
        parts += halves_of(table)
    return np.concatenate(parts, axis=0)


def back_constant():
    parts = []
    for placed in quadrant_tables():
        table = np.zeros((128, 128))
        for coord in range(3):
            at = coord * 25
            table[at : at + 25, at : at + 25] = placed
        parts += halves_of(table)
    return np.concatenate(parts, axis=0)


def dot(left, right):
    return lax.dot_general(left, right, (((1,), (0,)), ((), ())), preferred_element_type=F32)


def dot_nt(left, right):
    return lax.dot_general(left, right, (((1,), (1,)), ((), ())), preferred_element_type=F32)


def split(value):
    high = value.astype(BF16)
    return high, (value - high.astype(F32)).astype(BF16)


def triple(value, axis=1):
    high, low = split(value)
    return jnp.concatenate([high, low, high], axis=axis)


def tripled(constant, size, axis=0):
    parts = []
    for at in range(0, constant.shape[axis], 2 * size):
        high = lax.slice_in_dim(constant, at, at + size, axis=axis)
        low = lax.slice_in_dim(constant, at + size, at + 2 * size, axis=axis)
        parts += [high, high, low]
    return jnp.concatenate(parts, axis=axis)


def side_matrix(rows):
    return ones_where(iota((384, rows.shape[1]), 0) == rows)


def iota(shape, axis):
    return lax.broadcasted_iota(jnp.int32, shape, axis).astype(F32)


def ones_where(condition):
    return jnp.where(condition, 1.0, 0.0).astype(BF16)


def pick(blocks, key):
    chosen = blocks[0]
    for number in range(1, len(blocks)):
        chosen = jnp.where(key == float(number), blocks[number], chosen)
    return chosen


def lane_blocks(value, count):
    return [value[:, 128 * b : 128 * b + 128] for b in range(count)]


def positions(owner):
    records = owner.shape[1]
    column = columns_of(owner)[:, 0:1]
    same = (column == owner) & (iota((records, records), 0) < iota((records, records), 1))
    return owner * 2.0 + jnp.sum(jnp.where(same, 1.0, 0.0), axis=0, keepdims=True)


def columns_of(rows):
    count = rows.shape[1]
    eye = ones_where(iota((count, count), 0) == iota((count, count), 1))
    padded = jnp.broadcast_to(rows, (8, count)) if rows.shape[0] == 1 else rows
    return dot_nt(eye, padded.astype(BF16))


def child_table(pool, child_k):
    table = dot(triple(pool), tripled(child_k, 128))
    count = pool.shape[0] // 3
    stacked = [
        jnp.concatenate(
            [table[c * count : (c + 1) * count, o * 128 : o * 128 + 128] for c in range(3)], axis=1
        )
        for o in range(8)
    ]
    high, low = split(jnp.concatenate(stacked, axis=0))
    return jnp.concatenate([high.astype(F32), low.astype(F32)], axis=0).astype(BF16)


def row_picker(key, size):
    places = iota((key.shape[0], 2 * size), 1)
    places = jnp.where(places >= float(size), places - float(size), places)
    return ones_where(key == places)


def keys_of(parent, octant, filled):
    own = jnp.where(filled & (parent >= 0.0), octant * float(POOL) + parent, -1.0)
    halo = jnp.where(filled & (parent < 0.0), octant, -1.0)
    return own, halo


def slot_integers(ints, slots, position):
    hot = ones_where(iota((slots, position.shape[1]), 0) == position)
    return dot_nt(hot, ints.astype(BF16))


def requests(ints, pairs, position, scratch):
    records = ints.shape[1]
    scratch[...] = jnp.zeros(scratch.shape, F32)
    scratch[0:8, 0:records] = ints
    scratch[SECOND : SECOND + 8, records : 2 * records] = ints
    places = iota((pairs, records), 0) * 2.0
    hot = jnp.concatenate([ones_where(places == position), ones_where(places + 1.0 == position)], 1)
    return dot_nt(hot, scratch[...].astype(BF16))


def expanded(rows):
    pairs = rows.shape[0]
    slot, pair = iota((2 * pairs, pairs), 0), iota((2 * pairs, pairs), 1)
    first, second = ones_where(slot == 2.0 * pair), ones_where(slot == 2.0 * pair + 1.0)
    rows = rows.astype(BF16)
    both = dot(first, rows), pltpu.roll(dot(second, rows), SECOND, 1)
    return both[0] + both[1]


def messages(table, sides, carried):
    faces = dot(table, sides).astype(BF16)
    filled = carried[:, VALID : VALID + 1] > 0.5
    side = carried[:, FSIDE : FSIDE + 1]
    own, halo = keys_of(carried[:, PROW : PROW + 1], carried[:, OCT : OCT + 1], filled)
    face = pick(lane_blocks(dot(row_picker(own, 8 * POOL), faces), 6), side)
    return face, jnp.where(halo >= 0.0, side * 8.0 + halo, -1.0)


def halo_messages(halo_table, sides, keys):
    faces = dot(halo_table, sides)
    rows = [block[8 * h : 8 * h + 8] for h in range(2) for block in lane_blocks(faces, 6)]
    return dot(row_picker(keys, 48), jnp.concatenate(rows, axis=0).astype(BF16))


def determinants(table, halo_table, slope_k, own, halo):
    children = dot(row_picker(own, 8 * POOL), table) + dot(row_picker(halo, 8), halo_table)
    slope_k = tripled(slope_k, 128, 1)
    grads = [dot_nt(slope_k, triple(block)) for block in lane_blocks(children, 3)]
    g = [[grads[c][128 * d : 128 * d + 128] for c in range(3)] for d in range(3)]
    first = g[0][0] * (g[1][1] * g[2][2] - g[2][1] * g[1][2])
    second = g[1][0] * (g[0][1] * g[2][2] - g[2][1] * g[0][2])
    third = g[2][0] * (g[0][1] * g[1][2] - g[1][1] * g[0][2])
    return first - second + third


def coarse_faces(coarse, side_k):
    high, low = split(coarse.T)
    return jnp.concatenate([dot(high, side_k), dot(low, side_k)], axis=1).astype(BF16)


def coarse_rows(integers, faces):
    filled = integers[:, VALID : VALID + 1] > 0.5
    elem = jnp.where(filled, integers[:, ELEM : ELEM + 1], -1.0)
    side = integers[:, SIDE : SIDE + 1]
    hot = ones_where(elem == iota((integers.shape[0], faces.shape[0]), 1))
    blocks = lane_blocks(dot(hot, faces), 12)
    return pick(blocks[:6], side) + pick(blocks[6:], side)


def mortar(fine, coarse, quad, tangent_k):
    parts = [triple(fine)]
    for number in range(4):
        parts.append(triple(jnp.where(quad == float(number), coarse, 0.0)))
    tangents = dot(jnp.concatenate(parts, axis=1), tripled(tangent_k, 128))
    t1, t2 = tangents[:, :128], tangents[:, 128:]
    ahead = lambda value, count: pltpu.roll(value, 128 - 25 * count, 1)
    return ahead(t1, 1) * ahead(t2, 2) - ahead(t1, 2) * ahead(t2, 1)


def partial_sums(normal, integers, back_k, elements):
    slots = integers.shape[0]
    filled = integers[:, VALID : VALID + 1] > 0.5
    side, quad = integers[:, SIDE : SIDE + 1], integers[:, QUAD : QUAD + 1]
    key = side * float(elements) + integers[:, ELEM : ELEM + 1]
    key = jnp.where(filled, key, -1.0)
    parts = []
    for number in range(4):
        parts.append(triple(jnp.where(quad == float(number), normal, 0.0)))
    back = dot(jnp.concatenate(parts, axis=1), tripled(back_k, 128))
    high, low = split(back.T)
    hot = ones_where(key == iota((slots, 6 * elements), 1))
    both = dot(jnp.concatenate([high, low], axis=0), hot)
    return both[:128] + both[128:]


def face_rows(returned, position):
    hot = ones_where(iota((returned.shape[0], position.shape[1]), 0) == position)
    high, low = split(returned.T)
    both = dot(jnp.concatenate([high, low], axis=0), hot)
    return both[:128] + both[128:]


def fill_pool(pool, last, parents):
    pool[...] = jnp.zeros(pool.shape, F32)
    last[...] = jnp.zeros(last.shape, F32)
    for c in range(3):
        own = parents[c]
        own = own - own[:, MIDDLE : MIDDLE + 1]
        pool[c * POOL : (c + 1) * POOL, 0:125] = own
        last[c : c + 1, 0:125] = own[POOL - 1 :]


def fill_coarse(scratch, coarse):
    for c in range(3):
        scratch[c * 128 + 120 : c * 128 + 128, :] = jnp.zeros((8, coarse.shape[2]), F32)
        whole = coarse[c]
        scratch[c * 128 : c * 128 + 125, :] = whole - whole[MIDDLE : MIDDLE + 1]


def record_integers(parent, octant, elem, side, c_elem, c_side, quad):
    elements = parent.shape[1]
    both = jnp.concatenate([parent, octant, jnp.zeros((6, elements), F32)], axis=0)
    hot = ones_where(iota((elements, elem.shape[1]), 0) == elem)
    chosen = dot(both.astype(BF16), hot)
    rows = [jnp.ones_like(elem), c_elem, c_side, quad, side, chosen[0:1], chosen[1:2],
            jnp.zeros_like(elem)]
    turned = columns_of(both)
    keys = keys_of(turned[:, 0:1], turned[:, 1:2], turned[:, 1:2] >= 0.0)
    return jnp.concatenate(rows, axis=0), keys


def write_partials(partial_out, sums, elements):
    for c in range(3):
        for s in range(6):
            partial_out[c, s * 25 : s * 25 + 25, :] = sums[
                c * 25 : c * 25 + 25, s * elements : (s + 1) * elements
            ]


INPUTS = ("parent", "octant", "elem", "owner", "side", "c_elem", "c_side", "quad", "parents",
          "child_k", "side_k", "coarse", "slope_k", "tangent_k", "back_k")


def kernel(leaves, doms, groups, *refs):
    count = len(INPUTS)
    sources = refs[:count]
    jac_out, normals_out, partial_out = refs[count : count + 3]
    copies = refs[count + 3 : 2 * count + 3]
    (pool, last, halo_in, wide, scratch, ask_send, ask_here, fine_send, fine_here,
     coarse_send, coarse_here,
     in_sems, halo_sems, send_sems, ask_sems, fine_sems, coarse_sems) = refs[2 * count + 3 :]
    leaf, dom = lax.axis_index("leaf"), lax.axis_index("dom")
    ranks = leaves * doms
    me = leaf * doms + dom
    slots = 2 * ranks
    mesh_id = pl.DeviceIdType.MESH

    loads = {
        name: pltpu.make_async_copy(sources[at], copies[at], in_sems.at[at])
        for at, name in enumerate(INPUTS)
    }
    for name in INPUTS:
        loads[name].start()

    def load(name):
        loads[name].wait()
        return copies[INPUTS.index(name)]

    xs = max(doms // 16, 1)
    zs = doms // (2 * xs)
    at_x, at_z, core = dom // (2 * zs), lax.rem(dom // 2, zs), lax.rem(dom, 2)
    z_steps = sorted(range(zs), key=lambda step: -min(step, zs - step))
    by_z = [(step, lax.rem(at_z + step, zs) * 2) for step in z_steps]
    by_core = [(1, 1 - core), (0, core)]

    def others(ahead, act):
        there = lax.rem(leaf + ahead, leaves)

        def plane(step_x, skip):
            base = lax.rem(at_x + step_x, xs) * (2 * zs)
            for step_z, z_part in by_z:
                for step_core, core_part in by_core:
                    if not (skip and step_z == 0 and step_core == 0):
                        act(there, base + z_part + core_part)

        def body(number, carry):
            plane(number + xs // 2, False)
            return carry

        if ahead:
            lax.fori_loop(0, xs, body, 0)
        else:
            for number in range(xs):
                step_x = (number + xs // 2) % xs
                plane(step_x, step_x == 0)

    far_first = sorted(range(leaves), key=lambda step: -min(step, leaves - step))

    barrier = pltpu.get_barrier_semaphore()

    def greet(l, d):
        pl.semaphore_signal(barrier, inc=1, device_id=(l, d), device_id_type=mesh_id)

    for ahead in far_first:
        others(ahead, greet)

    def send_all(ahead, source, target, send_sem, recv_sem):
        def send(l, d):
            pltpu.make_async_remote_copy(
                src_ref=source.at[l * doms + d],
                dst_ref=target.at[me],
                send_sem=send_sem,
                recv_sem=recv_sem,
                device_id=(l, d),
                device_id_type=mesh_id,
            ).start()

        others(ahead, send)

    def wait_rows(ref, rows, sem):
        most = ref.at[pl.ds(0, rows)]
        pltpu.make_async_copy(most, most, sem).wait()

    def wait_leaf(ref, back, sems):
        wait_rows(ref, doms if back else doms - 1, sems.at[back])

    names = ("parent", "octant", "elem", "side", "c_elem", "c_side", "quad")
    ints, keys = record_integers(*[load(name)[...].astype(F32) for name in names])
    position = positions(load("owner")[...].astype(F32))
    ask_send[...] = requests(ints, ranks, position, wide).reshape(ask_send.shape)
    carried = slot_integers(ints, slots, position)
    fill_pool(pool, last, load("parents"))
    child_k = load("child_k")[...]
    table = child_table(pool[...], child_k)
    sides = side_matrix(load("side_k")[...])
    fine, fine_keys = messages(table, sides, carried)

    pl.semaphore_wait(barrier, ranks - 1)
    after = lax.rem(me + 1, ranks)
    halo = pltpu.make_async_remote_copy(
        src_ref=last,
        dst_ref=halo_in,
        send_sem=halo_sems.at[0],
        recv_sem=halo_sems.at[1],
        device_id=(after // doms, lax.rem(after, doms)),
        device_id_type=mesh_id,
    )
    halo.start()
    for ahead in far_first:
        send_all(ahead, ask_send, ask_here, send_sems.at[0], ask_sems.at[ahead])
    ask_here[pl.ds(me, 1)] = ask_send[pl.ds(me, 1)]
    halo.wait()
    halo_table = child_table(jnp.concatenate([halo_in[c : c + 1] for c in range(3)], axis=0), child_k)
    fine = fine + halo_messages(halo_table, sides, fine_keys)
    fine_send[...] = fine.reshape(fine_send.shape)
    for ahead in far_first:
        send_all(ahead, fine_send, fine_here, send_sems.at[1], fine_sems.at[ahead])
    fine_here[pl.ds(me, 1)] = fine_send[pl.ds(me, 1)]

    coarse = load("coarse")
    elements = coarse.shape[2]
    fill_coarse(scratch, coarse)
    faces = coarse_faces(scratch[...], sides)
    tangent_k = load("tangent_k")[...]
    back_k = load("back_k")[...]
    slope_k = load("slope_k")[...]

    asked = []
    for group in groups:
        starts = [lax.rem(leaf + leaves - back, leaves) * doms for back in group]
        for back in group:
            wait_leaf(ask_here, back, ask_sems)
        for start in starts:
            rows = ask_here[pl.ds(start, doms)].reshape(doms, 128)
            asked.append(expanded(rows))
        rows = coarse_rows(jnp.concatenate(asked[-len(group) :], axis=0), faces)
        for number, start in enumerate(starts):
            mine = rows[number * 2 * doms : (number + 1) * 2 * doms]
            coarse_send[pl.ds(start, doms)] = mine.reshape(doms, 2, 128)
        for back in group:
            ahead = (leaves - back) % leaves
            send_all(ahead, coarse_send, coarse_here, send_sems.at[2], coarse_sems.at[ahead])
    coarse_here[pl.ds(me, 1)] = coarse_send[pl.ds(me, 1)]

    jac_out[...] = determinants(table, halo_table, slope_k, *keys)[0:125]

    order = [back for group in groups for back in group]
    starts = [lax.rem(leaf + leaves - back, leaves) * doms for back in order]
    part = lambda ref: jnp.concatenate(
        [ref[pl.ds(start, doms)].reshape(2 * doms, 128) for start in starts], axis=0
    )
    for back in order:
        wait_leaf(fine_here, back, fine_sems)
    asked = jnp.concatenate(asked, axis=0)
    normal = mortar(part(fine_here), part(coarse_send), asked[:, QUAD : QUAD + 1], tangent_k)
    write_partials(partial_out, partial_sums(normal, asked, back_k, elements), elements)

    for back in order:
        wait_leaf(coarse_here, back, coarse_sems)
    normal = mortar(
        fine, coarse_here[...].reshape(slots, 128), carried[:, QUAD : QUAD + 1], tangent_k
    )
    returned = face_rows(normal, position)
    for c in range(3):
        normals_out[c] = returned[c * 25 : c * 25 + 25]
    for at, ref in enumerate((ask_send, fine_send, coarse_send)):
        wait_rows(ref, ranks - 1, send_sems.at[at])


def shards(parents, coarse, parent, octant, elem, side, owner, c_elem, c_side, quad):
    leaves, doms = lax.axis_size("leaf"), lax.axis_size("dom")
    ranks = leaves * doms
    records, elements = elem.shape[0], parent.shape[0]
    row = lambda value: value.reshape(1, -1)
    given = dict(
        parent=row(parent), octant=row(octant), elem=row(elem), side=row(side), owner=row(owner),
        c_elem=row(c_elem), c_side=row(c_side), quad=row(quad),
        parents=parents.transpose(0, 2, 1), coarse=coarse,
        child_k=jnp.asarray(child_constant()), side_k=jnp.asarray(side_constant()),
        slope_k=jnp.asarray(slope_constant()), tangent_k=jnp.asarray(tangent_constant()),
        back_k=jnp.asarray(back_constant()),
    )
    args = [pltpu.with_memory_space_constraint(given[name], pltpu.HBM) for name in INPUTS]
    buffer = pltpu.VMEM((ranks, 2, 128), F32)
    request = pltpu.VMEM((ranks, 1, 128), F32)
    far_first = sorted(range(leaves), key=lambda step: -min(step, leaves - step))
    groups = [far_first[at : at + GROUP] for at in range(0, leaves, GROUP)]
    shapes = (
        jax.ShapeDtypeStruct((125, elements), F32),
        jax.ShapeDtypeStruct((3, 25, records), F32),
        jax.ShapeDtypeStruct((3, 150, coarse.shape[2]), F32),
    )
    return pl.pallas_call(
        functools.partial(kernel, leaves, doms, groups),
        out_shape=shapes,
        in_specs=[pl.BlockSpec(memory_space=pltpu.HBM)] * len(args),
        out_specs=[pl.BlockSpec(memory_space=pltpu.VMEM)] * 3,
        scratch_shapes=[pltpu.VMEM(arg.shape, arg.dtype) for arg in args] + [
            pltpu.VMEM((3 * POOL, 128), F32),
            pltpu.VMEM((8, 128), F32),
            pltpu.VMEM((8, 128), F32),
            pltpu.VMEM((128, 2 * records), F32),
            pltpu.VMEM((384, coarse.shape[2]), F32),
            request, request, buffer, buffer, buffer, buffer,
            pltpu.SemaphoreType.DMA((len(args),)),
            pltpu.SemaphoreType.DMA((2,)),
            pltpu.SemaphoreType.DMA((3,)),
            pltpu.SemaphoreType.DMA((leaves,)),
            pltpu.SemaphoreType.DMA((leaves,)),
            pltpu.SemaphoreType.DMA((leaves,)),
        ],
        compiler_params=pltpu.CompilerParams(
            collective_id=0, has_side_effects=True, vmem_limit_bytes=40 << 20
        ),
    )(*args)


def solution(mesh):
    whole = P(None, None, ("leaf", "dom"))
    line = P(("leaf", "dom"))
    return jax.shard_map(
        shards,
        mesh=mesh,
        in_specs=(whole, whole, line, line, line, line, P(("leaf", "dom"), None), line, line, line),
        out_specs=(P(None, ("leaf", "dom")), whole, whole),
        check_vma=False,
    )
```

```python
import functools
import math

import jax
import jax.numpy as jnp
import ml_dtypes
import numpy as np
from jax import lax
from jax.experimental import pallas as pl
from jax.experimental.pallas import tpu as pltpu
from jax.sharding import PartitionSpec as P

F32 = jnp.float32
BF16 = jnp.bfloat16
POOL = 32
MIDDLE = 62
GROUP = 1
VALID, ELEM, SIDE, QUAD, FSIDE, PROW, OCT = range(7)
SECOND = 64


def lobatto_nodes():
    return np.array([-1.0, -math.sqrt(3.0 / 7.0), 0.0, math.sqrt(3.0 / 7.0), 1.0])


def lagrange_table(targets):
    points = lobatto_nodes()
    table = np.ones((targets.shape[0], 5))
    for column in range(5):
        for others in range(5):
            if others != column:
                table[:, column] *= (targets - points[others]) / (points[column] - points[others])
    return table


def derivative_table():
    points = lobatto_nodes()
    table = np.zeros((5, 5))
    for target in range(5):
        for column in range(5):
            total = 0.0
            for others in range(5):
                if others != column:
                    term = 1.0 / (points[column] - points[others])
                    for remain in range(5):
                        if remain != column and remain != others:
                            term *= (points[target] - points[remain]) / (
                                points[column] - points[remain]
                            )
                    total += term
            table[target, column] = total
    return table


def f32_table(table):
    return table.astype(np.float32).astype(np.float64)


LOWER = f32_table(lagrange_table((lobatto_nodes() - 1.0) / 2.0))
UPPER = f32_table(lagrange_table((lobatto_nodes() + 1.0) / 2.0))
SLOPE = f32_table(derivative_table())
EYE = np.eye(5)


def halves_of(table):
    high = table.astype(np.float32).astype(ml_dtypes.bfloat16)
    low = (table - high.astype(np.float64)).astype(np.float32).astype(ml_dtypes.bfloat16)
    return high, low


def side_nodes(side):
    direction, level = side // 2, side % 2 * 4
    fixed = (25, 5, 1)[direction]
    first = 5 if direction == 0 else 25
    second = 5 if direction == 2 else 1
    return [level * fixed + a * first + b * second for a in range(5) for b in range(5)]


def child_constant():
    table = np.zeros((128, 8 * 128))
    for octant in range(8):
        picks = [UPPER if octant & bit else LOWER for bit in (4, 2, 1)]
        whole = np.kron(np.kron(picks[0], picks[1]), picks[2])
        table[:125, octant * 128 : octant * 128 + 125] = whole.T
    return np.concatenate(halves_of(table), axis=0)


def slope_constant():
    table = np.zeros((384, 128))
    for direction in range(3):
        picks = [SLOPE if axis == direction else EYE for axis in range(3)]
        whole = np.kron(np.kron(picks[0], picks[1]), picks[2])
        table[direction * 128 : direction * 128 + 125, :125] = whole
    return np.concatenate(halves_of(table), axis=1)


def side_constant():
    rows = np.full((1, 768), -1.0, np.float32)
    for side in range(6):
        for coord in range(3):
            at = side * 128 + coord * 25
            rows[0, at : at + 25] = [coord * 128 + node for node in side_nodes(side)]
    return rows


def quadrant_tables():
    for quadrant in range(4):
        first = UPPER if quadrant & 2 else LOWER
        second = UPPER if quadrant & 1 else LOWER
        yield np.kron(first, second)


def tangent_constant():
    slopes = [np.kron(SLOPE, EYE), np.kron(EYE, SLOPE)]
    parts = []
    for placed in [np.eye(25)] + list(quadrant_tables()):
        table = np.zeros((128, 256))
        for which, slope in enumerate(slopes):
            whole = 0.5 * (slope @ placed)
            for spot, coord in enumerate((0, 1, 2, 0, 1)):
                at = which * 128 + spot * 25
                table[coord * 25 : coord * 25 + 25, at : at + 25] = whole.T
        parts += halves_of(table)
    return np.concatenate(parts, axis=0)


def back_constant():
    parts = []
    for placed in quadrant_tables():
        table = np.zeros((128, 128))
        for coord in range(3):
            at = coord * 25
            table[at : at + 25, at : at + 25] = placed
        parts += halves_of(table)
    return np.concatenate(parts, axis=0)


def dot(left, right):
    return lax.dot_general(left, right, (((1,), (0,)), ((), ())), preferred_element_type=F32)


def dot_nt(left, right):
    return lax.dot_general(left, right, (((1,), (1,)), ((), ())), preferred_element_type=F32)


def split(value):
    high = value.astype(BF16)
    return high, (value - high.astype(F32)).astype(BF16)


def triple(value, axis=1):
    high, low = split(value)
    return jnp.concatenate([high, low, high], axis=axis)


def tripled(constant, size, axis=0):
    parts = []
    for at in range(0, constant.shape[axis], 2 * size):
        high = lax.slice_in_dim(constant, at, at + size, axis=axis)
        low = lax.slice_in_dim(constant, at + size, at + 2 * size, axis=axis)
        parts += [high, high, low]
    return jnp.concatenate(parts, axis=axis)


def side_matrix(rows):
    return ones_where(iota((384, rows.shape[1]), 0) == rows)


def iota(shape, axis):
    return lax.broadcasted_iota(jnp.int32, shape, axis).astype(F32)


def ones_where(condition):
    return jnp.where(condition, 1.0, 0.0).astype(BF16)


def pick(blocks, key):
    chosen = blocks[0]
    for number in range(1, len(blocks)):
        chosen = jnp.where(key == float(number), blocks[number], chosen)
    return chosen


def lane_blocks(value, count):
    return [value[:, 128 * b : 128 * b + 128] for b in range(count)]


def positions(owner):
    records = owner.shape[1]
    column = columns_of(owner)[:, 0:1]
    same = (column == owner) & (iota((records, records), 0) < iota((records, records), 1))
    rank = jnp.sum(jnp.where(same, 1.0, 0.0), axis=0, keepdims=True)
    return owner * 2.0 + rank, column * 2.0 + columns_of(rank)[:, 0:1]


def columns_of(rows):
    count = rows.shape[1]
    eye = ones_where(iota((count, count), 0) == iota((count, count), 1))
    padded = jnp.broadcast_to(rows, (8, count)) if rows.shape[0] == 1 else rows
    return dot_nt(eye, padded.astype(BF16))


def child_table(pool, child_k):
    table = dot(triple(pool), tripled(child_k, 128))
    count = pool.shape[0] // 3
    stacked = [
        jnp.concatenate(
            [table[c * count : (c + 1) * count, o * 128 : o * 128 + 128] for c in range(3)], axis=1
        )
        for o in range(8)
    ]
    high, low = split(jnp.concatenate(stacked, axis=0))
    return jnp.concatenate([high.astype(F32), low.astype(F32)], axis=0).astype(BF16)


def row_picker(key, size):
    places = iota((key.shape[0], 2 * size), 1)
    places = jnp.where(places >= float(size), places - float(size), places)
    return ones_where(key == places)


def keys_of(parent, octant, filled):
    own = jnp.where(filled & (parent >= 0.0), octant * float(POOL) + parent, -1.0)
    halo = jnp.where(filled & (parent < 0.0), octant, -1.0)
    return own, halo


def slot_integers(ints, slots, position):
    hot = ones_where(iota((slots, position.shape[1]), 0) == position)
    return dot_nt(hot, ints.astype(BF16))


def requests(ints, pairs, position, scratch):
    records = ints.shape[1]
    scratch[...] = jnp.zeros(scratch.shape, F32)
    scratch[0:8, 0:records] = ints
    scratch[SECOND : SECOND + 8, records : 2 * records] = ints
    places = iota((pairs, records), 0) * 2.0
    hot = jnp.concatenate([ones_where(places == position), ones_where(places + 1.0 == position)], 1)
    return dot_nt(hot, scratch[...].astype(BF16))


def expanded(rows):
    pairs = rows.shape[0]
    slot, pair = iota((2 * pairs, pairs), 0), iota((2 * pairs, pairs), 1)
    first, second = ones_where(slot == 2.0 * pair), ones_where(slot == 2.0 * pair + 1.0)
    rows = rows.astype(BF16)
    both = dot(first, rows), pltpu.roll(dot(second, rows), SECOND, 1)
    return both[0] + both[1]


def messages(table, sides, carried):
    faces = dot(table, sides).astype(BF16)
    filled = carried[:, VALID : VALID + 1] > 0.5
    side = carried[:, FSIDE : FSIDE + 1]
    own, halo = keys_of(carried[:, PROW : PROW + 1], carried[:, OCT : OCT + 1], filled)
    face = pick(lane_blocks(dot(row_picker(own, 8 * POOL), faces), 6), side)
    return face, jnp.where(halo >= 0.0, side * 8.0 + halo, -1.0)


def halo_messages(halo_table, sides, keys):
    faces = dot(halo_table, sides)
    rows = [block[8 * h : 8 * h + 8] for h in range(2) for block in lane_blocks(faces, 6)]
    return dot(row_picker(keys, 48), jnp.concatenate(rows, axis=0).astype(BF16))


def determinants(table, halo_table, slope_k, own, halo):
    children = dot(row_picker(own, 8 * POOL), table) + dot(row_picker(halo, 8), halo_table)
    slope_k = tripled(slope_k, 128, 1)
    grads = [dot_nt(slope_k, triple(block)) for block in lane_blocks(children, 3)]
    g = [[grads[c][128 * d : 128 * d + 128] for c in range(3)] for d in range(3)]
    first = g[0][0] * (g[1][1] * g[2][2] - g[2][1] * g[1][2])
    second = g[1][0] * (g[0][1] * g[2][2] - g[2][1] * g[0][2])
    third = g[2][0] * (g[0][1] * g[1][2] - g[1][1] * g[0][2])
    return first - second + third


def coarse_faces(coarse, side_k):
    high, low = split(coarse.T)
    return jnp.concatenate([dot(high, side_k), dot(low, side_k)], axis=1).astype(BF16)


def coarse_rows(integers, faces):
    filled = integers[:, VALID : VALID + 1] > 0.5
    elem = jnp.where(filled, integers[:, ELEM : ELEM + 1], -1.0)
    side = integers[:, SIDE : SIDE + 1]
    hot = ones_where(elem == iota((integers.shape[0], faces.shape[0]), 1))
    blocks = lane_blocks(dot(hot, faces), 12)
    return pick(blocks[:6], side) + pick(blocks[6:], side)


def mortar(fine, coarse, quad, tangent_k):
    parts = [triple(fine)]
    for number in range(4):
        parts.append(triple(jnp.where(quad == float(number), coarse, 0.0)))
    tangents = dot(jnp.concatenate(parts, axis=1), tripled(tangent_k, 128))
    t1, t2 = tangents[:, :128], tangents[:, 128:]
    ahead = lambda value, count: pltpu.roll(value, 128 - 25 * count, 1)
    return ahead(t1, 1) * ahead(t2, 2) - ahead(t1, 2) * ahead(t2, 1)


def partial_sums(normal, integers, back_k, elements):
    slots = integers.shape[0]
    filled = integers[:, VALID : VALID + 1] > 0.5
    side, quad = integers[:, SIDE : SIDE + 1], integers[:, QUAD : QUAD + 1]
    key = side * float(elements) + integers[:, ELEM : ELEM + 1]
    key = jnp.where(filled, key, -1.0)
    parts = []
    for number in range(4):
        parts.append(triple(jnp.where(quad == float(number), normal, 0.0)))
    back = dot(jnp.concatenate(parts, axis=1), tripled(back_k, 128))
    high, low = split(back.T)
    hot = ones_where(key == iota((slots, 6 * elements), 1))
    both = dot(jnp.concatenate([high, low], axis=0), hot)
    return both[:128] + both[128:]


def by_record(slot_rows, places):
    high, low = split(slot_rows)
    hot = ones_where(places == iota((places.shape[0], slot_rows.shape[0]), 1))
    both = dot(hot, jnp.concatenate([high, low], axis=1))
    return both[:, :128] + both[:, 128:]


def fill_pool(pool, last, parents):
    pool[...] = jnp.zeros(pool.shape, F32)
    last[...] = jnp.zeros(last.shape, F32)
    for c in range(3):
        own = parents[c]
        own = own - own[:, MIDDLE : MIDDLE + 1]
        pool[c * POOL : (c + 1) * POOL, 0:125] = own
        last[c : c + 1, 0:125] = own[POOL - 1 :]


def fill_coarse(scratch, coarse):
    for c in range(3):
        scratch[c * 128 + 120 : c * 128 + 128, :] = jnp.zeros((8, coarse.shape[2]), F32)
        whole = coarse[c]
        scratch[c * 128 : c * 128 + 125, :] = whole - whole[MIDDLE : MIDDLE + 1]


def record_integers(parent, octant, elem, side, c_elem, c_side, quad):
    elements = parent.shape[1]
    both = jnp.concatenate([parent, octant, jnp.zeros((6, elements), F32)], axis=0)
    hot = ones_where(iota((elements, elem.shape[1]), 0) == elem)
    chosen = dot(both.astype(BF16), hot)
    rows = [jnp.ones_like(elem), c_elem, c_side, quad, side, chosen[0:1], chosen[1:2],
            jnp.zeros_like(elem)]
    turned = columns_of(both)
    keys = keys_of(turned[:, 0:1], turned[:, 1:2], turned[:, 1:2] >= 0.0)
    return jnp.concatenate(rows, axis=0), keys


def write_partials(partial_out, sums, elements):
    for c in range(3):
        for s in range(6):
            partial_out[c, s * 25 : s * 25 + 25, :] = sums[
                c * 25 : c * 25 + 25, s * elements : (s + 1) * elements
            ]


INPUTS = ("parent", "octant", "elem", "owner", "side", "c_elem", "c_side", "quad", "parents",
          "child_k", "side_k", "coarse", "slope_k", "tangent_k", "back_k")


def kernel(leaves, doms, groups, *refs):
    count = len(INPUTS)
    sources = refs[:count]
    jac_out, normals_out, partial_out = refs[count : count + 3]
    copies = refs[count + 3 : 2 * count + 3]
    (pool, last, halo_in, wide, scratch, ask_send, ask_here, fine_send, fine_here,
     coarse_send, coarse_here,
     in_sems, halo_sems, send_sems, ask_sems, fine_sems, coarse_sems) = refs[2 * count + 3 :]
    leaf, dom = lax.axis_index("leaf"), lax.axis_index("dom")
    ranks = leaves * doms
    me = leaf * doms + dom
    slots = 2 * ranks
    mesh_id = pl.DeviceIdType.MESH

    loads = {
        name: pltpu.make_async_copy(sources[at], copies[at], in_sems.at[at])
        for at, name in enumerate(INPUTS)
    }
    for name in INPUTS:
        loads[name].start()

    def load(name):
        loads[name].wait()
        return copies[INPUTS.index(name)]

    xs = max(doms // 16, 1)
    zs = doms // (2 * xs)
    at_x, at_z, core = dom // (2 * zs), lax.rem(dom // 2, zs), lax.rem(dom, 2)
    z_steps = sorted(range(zs), key=lambda step: -min(step, zs - step))
    by_z = [(step, lax.rem(at_z + step, zs) * 2) for step in z_steps]
    by_core = [(1, 1 - core), (0, core)]

    def others(ahead, act):
        there = lax.rem(leaf + ahead, leaves)

        def plane(step_x, skip):
            base = lax.rem(at_x + step_x, xs) * (2 * zs)
            for step_z, z_part in by_z:
                for step_core, core_part in by_core:
                    if not (skip and step_z == 0 and step_core == 0):
                        act(there, base + z_part + core_part)

        def body(number, carry):
            plane(number + xs // 2, False)
            return carry

        if ahead:
            lax.fori_loop(0, xs, body, 0)
        else:
            for number in range(xs):
                step_x = (number + xs // 2) % xs
                plane(step_x, step_x == 0)

    far_first = sorted(range(leaves), key=lambda step: -min(step, leaves - step))

    barrier = pltpu.get_barrier_semaphore()

    def greet(l, d):
        pl.semaphore_signal(barrier, inc=1, device_id=(l, d), device_id_type=mesh_id)

    for ahead in far_first:
        others(ahead, greet)

    def send_all(ahead, source, target, send_sem, recv_sem):
        def send(l, d):
            pltpu.make_async_remote_copy(
                src_ref=source.at[l * doms + d],
                dst_ref=target.at[me],
                send_sem=send_sem,
                recv_sem=recv_sem,
                device_id=(l, d),
                device_id_type=mesh_id,
            ).start()

        others(ahead, send)

    def wait_rows(ref, rows, sem):
        most = ref.at[pl.ds(0, rows)]
        pltpu.make_async_copy(most, most, sem).wait()

    def wait_leaf(ref, back, sems):
        wait_rows(ref, doms if back else doms - 1, sems.at[back])

    names = ("parent", "octant", "elem", "side", "c_elem", "c_side", "quad")
    ints, keys = record_integers(*[load(name)[...].astype(F32) for name in names])
    position, places = positions(load("owner")[...].astype(F32))
    ask_send[...] = requests(ints, ranks, position, wide).reshape(ask_send.shape)
    carried = slot_integers(ints, slots, position)
    fill_pool(pool, last, load("parents"))
    child_k = load("child_k")[...]
    table = child_table(pool[...], child_k)
    sides = side_matrix(load("side_k")[...])
    fine, fine_keys = messages(table, sides, carried)

    coarse = load("coarse")
    elements = coarse.shape[2]
    fill_coarse(scratch, coarse)
    faces = coarse_faces(scratch[...], sides)

    pl.semaphore_wait(barrier, ranks - 1)
    after = lax.rem(me + 1, ranks)
    halo = pltpu.make_async_remote_copy(
        src_ref=last,
        dst_ref=halo_in,
        send_sem=halo_sems.at[0],
        recv_sem=halo_sems.at[1],
        device_id=(after // doms, lax.rem(after, doms)),
        device_id_type=mesh_id,
    )
    halo.start()
    for ahead in far_first:
        send_all(ahead, ask_send, ask_here, send_sems.at[0], ask_sems.at[ahead])
    ask_here[pl.ds(me, 1)] = ask_send[pl.ds(me, 1)]
    halo.wait()
    halo_table = child_table(jnp.concatenate([halo_in[c : c + 1] for c in range(3)], axis=0), child_k)
    fine = fine + halo_messages(halo_table, sides, fine_keys)
    fine_send[...] = fine.reshape(fine_send.shape)
    for ahead in far_first:
        send_all(ahead, fine_send, fine_here, send_sems.at[1], fine_sems.at[ahead])
    fine_here[pl.ds(me, 1)] = fine_send[pl.ds(me, 1)]

    tangent_k = load("tangent_k")[...]
    back_k = load("back_k")[...]
    slope_k = load("slope_k")[...]

    asked = []
    for group in groups:
        starts = [lax.rem(leaf + leaves - back, leaves) * doms for back in group]
        for back in group:
            wait_leaf(ask_here, back, ask_sems)
        for start in starts:
            rows = ask_here[pl.ds(start, doms)].reshape(doms, 128)
            asked.append(expanded(rows))
        rows = coarse_rows(jnp.concatenate(asked[-len(group) :], axis=0), faces)
        for number, start in enumerate(starts):
            mine = rows[number * 2 * doms : (number + 1) * 2 * doms]
            coarse_send[pl.ds(start, doms)] = mine.reshape(doms, 2, 128)
        for back in group:
            ahead = (leaves - back) % leaves
            send_all(ahead, coarse_send, coarse_here, send_sems.at[2], coarse_sems.at[ahead])
    coarse_here[pl.ds(me, 1)] = coarse_send[pl.ds(me, 1)]

    jac_out[...] = determinants(table, halo_table, slope_k, *keys)[0:125]

    order = [back for group in groups for back in group]
    starts = [lax.rem(leaf + leaves - back, leaves) * doms for back in order]
    part = lambda ref: jnp.concatenate(
        [ref[pl.ds(start, doms)].reshape(2 * doms, 128) for start in starts], axis=0
    )
    for back in order:
        wait_leaf(fine_here, back, fine_sems)
    asked = jnp.concatenate(asked, axis=0)
    normal = mortar(part(fine_here), part(coarse_send), asked[:, QUAD : QUAD + 1], tangent_k)
    write_partials(partial_out, partial_sums(normal, asked, back_k, elements), elements)

    fine = by_record(fine, places)
    quad = columns_of(ints)[:, QUAD : QUAD + 1]
    for back in order:
        wait_leaf(coarse_here, back, coarse_sems)
    coarse = by_record(coarse_here[...].reshape(slots, 128), places)
    turned = mortar(fine, coarse, quad, tangent_k).T
    for c in range(3):
        normals_out[c] = turned[c * 25 : c * 25 + 25]
    for at, ref in enumerate((ask_send, fine_send, coarse_send)):
        wait_rows(ref, ranks - 1, send_sems.at[at])


def store_kernel(*refs):
    count = (len(refs) - 1) // 2
    copies = [
        pltpu.make_async_copy(refs[at], refs[count + at], refs[-1].at[at]) for at in range(count)
    ]
    for copy in copies:
        copy.start()
    for copy in copies:
        copy.wait()


def shards(parents, coarse, parent, octant, elem, side, owner, c_elem, c_side, quad):
    leaves, doms = lax.axis_size("leaf"), lax.axis_size("dom")
    ranks = leaves * doms
    records, elements = elem.shape[0], parent.shape[0]
    row = lambda value: value.reshape(1, -1)
    given = dict(
        parent=row(parent), octant=row(octant), elem=row(elem), side=row(side), owner=row(owner),
        c_elem=row(c_elem), c_side=row(c_side), quad=row(quad),
        parents=parents.transpose(0, 2, 1), coarse=coarse,
        child_k=jnp.asarray(child_constant()), side_k=jnp.asarray(side_constant()),
        slope_k=jnp.asarray(slope_constant()), tangent_k=jnp.asarray(tangent_constant()),
        back_k=jnp.asarray(back_constant()),
    )
    args = [pltpu.with_memory_space_constraint(given[name], pltpu.HBM) for name in INPUTS]
    buffer = pltpu.VMEM((ranks, 2, 128), F32)
    request = pltpu.VMEM((ranks, 1, 128), F32)
    far_first = sorted(range(leaves), key=lambda step: -min(step, leaves - step))
    groups = [far_first[at : at + GROUP] for at in range(0, leaves, GROUP)]
    shapes = (
        jax.ShapeDtypeStruct((125, elements), F32),
        jax.ShapeDtypeStruct((3, 25, records), F32),
        jax.ShapeDtypeStruct((3, 150, coarse.shape[2]), F32),
    )
    results = pl.pallas_call(
        functools.partial(kernel, leaves, doms, groups),
        out_shape=shapes,
        in_specs=[pl.BlockSpec(memory_space=pltpu.HBM)] * len(args),
        out_specs=[pl.BlockSpec(memory_space=pltpu.VMEM)] * 3,
        scratch_shapes=[pltpu.VMEM(arg.shape, arg.dtype) for arg in args] + [
            pltpu.VMEM((3 * POOL, 128), F32),
            pltpu.VMEM((8, 128), F32),
            pltpu.VMEM((8, 128), F32),
            pltpu.VMEM((128, 2 * records), F32),
            pltpu.VMEM((384, coarse.shape[2]), F32),
            request, request, buffer, buffer, buffer, buffer,
            pltpu.SemaphoreType.DMA((len(args),)),
            pltpu.SemaphoreType.DMA((2,)),
            pltpu.SemaphoreType.DMA((3,)),
            pltpu.SemaphoreType.DMA((leaves,)),
            pltpu.SemaphoreType.DMA((leaves,)),
            pltpu.SemaphoreType.DMA((leaves,)),
        ],
        compiler_params=pltpu.CompilerParams(
            collective_id=0, has_side_effects=True, vmem_limit_bytes=40 << 20
        ),
    )(*args)
    return pl.pallas_call(
        store_kernel,
        out_shape=shapes,
        in_specs=[pl.BlockSpec(memory_space=pl.ANY)] * 3,
        out_specs=[pl.BlockSpec(memory_space=pltpu.HBM)] * 3,
        scratch_shapes=[pltpu.SemaphoreType.DMA((3,))],
        compiler_params=pltpu.CompilerParams(vmem_limit_bytes=4 << 20),
    )(*results)


def solution(mesh):
    whole = P(None, None, ("leaf", "dom"))
    line = P(("leaf", "dom"))
    return jax.shard_map(
        shards,
        mesh=mesh,
        in_specs=(whole, whole, line, line, line, line, P(("leaf", "dom"), None), line, line, line),
        out_specs=(P(None, ("leaf", "dom")), whole, whole),
        check_vma=False,
    )
```

```python
import functools
import math

import jax
import jax.numpy as jnp
import ml_dtypes
import numpy as np
from jax import lax
from jax.experimental import pallas as pl
from jax.experimental.pallas import tpu as pltpu
from jax.sharding import PartitionSpec as P

F32 = jnp.float32
BF16 = jnp.bfloat16
POOL = 32
MIDDLE = 62
GROUP = 1
VALID, ELEM, SIDE, QUAD, FSIDE, PROW, OCT = range(7)
SECOND = 64


def lobatto_nodes():
    return np.array([-1.0, -math.sqrt(3.0 / 7.0), 0.0, math.sqrt(3.0 / 7.0), 1.0])


def lagrange_table(targets):
    points = lobatto_nodes()
    table = np.ones((targets.shape[0], 5))
    for column in range(5):
        for others in range(5):
            if others != column:
                table[:, column] *= (targets - points[others]) / (points[column] - points[others])
    return table


def derivative_table():
    points = lobatto_nodes()
    table = np.zeros((5, 5))
    for target in range(5):
        for column in range(5):
            total = 0.0
            for others in range(5):
                if others != column:
                    term = 1.0 / (points[column] - points[others])
                    for remain in range(5):
                        if remain != column and remain != others:
                            term *= (points[target] - points[remain]) / (
                                points[column] - points[remain]
                            )
                    total += term
            table[target, column] = total
    return table


def f32_table(table):
    return table.astype(np.float32).astype(np.float64)


LOWER = f32_table(lagrange_table((lobatto_nodes() - 1.0) / 2.0))
UPPER = f32_table(lagrange_table((lobatto_nodes() + 1.0) / 2.0))
SLOPE = f32_table(derivative_table())
EYE = np.eye(5)


def halves_of(table):
    high = table.astype(np.float32).astype(ml_dtypes.bfloat16)
    low = (table - high.astype(np.float64)).astype(np.float32).astype(ml_dtypes.bfloat16)
    return high, low


def side_nodes(side):
    direction, level = side // 2, side % 2 * 4
    fixed = (25, 5, 1)[direction]
    first = 5 if direction == 0 else 25
    second = 5 if direction == 2 else 1
    return [level * fixed + a * first + b * second for a in range(5) for b in range(5)]


def child_constant():
    table = np.zeros((128, 8 * 128))
    for octant in range(8):
        picks = [UPPER if octant & bit else LOWER for bit in (4, 2, 1)]
        whole = np.kron(np.kron(picks[0], picks[1]), picks[2])
        table[:125, octant * 128 : octant * 128 + 125] = whole.T
    return np.concatenate(halves_of(table), axis=0)


def slope_constant():
    table = np.zeros((384, 128))
    for direction in range(3):
        picks = [SLOPE if axis == direction else EYE for axis in range(3)]
        whole = np.kron(np.kron(picks[0], picks[1]), picks[2])
        table[direction * 128 : direction * 128 + 125, :125] = whole
    return np.concatenate(halves_of(table), axis=1)


def side_constant():
    rows = np.full((1, 768), -1.0, np.float32)
    for side in range(6):
        for coord in range(3):
            at = side * 128 + coord * 25
            rows[0, at : at + 25] = [coord * 128 + node for node in side_nodes(side)]
    return rows


def quadrant_tables():
    for quadrant in range(4):
        first = UPPER if quadrant & 2 else LOWER
        second = UPPER if quadrant & 1 else LOWER
        yield np.kron(first, second)


def tangent_constant():
    slopes = [np.kron(SLOPE, EYE), np.kron(EYE, SLOPE)]
    parts = []
    for placed in [np.eye(25)] + list(quadrant_tables()):
        table = np.zeros((128, 256))
        for which, slope in enumerate(slopes):
            whole = 0.5 * (slope @ placed)
            for spot, coord in enumerate((0, 1, 2, 0, 1)):
                at = which * 128 + spot * 25
                table[coord * 25 : coord * 25 + 25, at : at + 25] = whole.T
        parts += halves_of(table)
    return np.concatenate(parts, axis=0)


def back_constant():
    parts = []
    for placed in quadrant_tables():
        table = np.zeros((128, 128))
        for coord in range(3):
            at = coord * 25
            table[at : at + 25, at : at + 25] = placed
        parts += halves_of(table)
    return np.concatenate(parts, axis=0)


def dot(left, right):
    return lax.dot_general(left, right, (((1,), (0,)), ((), ())), preferred_element_type=F32)


def dot_nt(left, right):
    return lax.dot_general(left, right, (((1,), (1,)), ((), ())), preferred_element_type=F32)


def split(value):
    high = value.astype(BF16)
    return high, (value - high.astype(F32)).astype(BF16)


def triple(value, axis=1):
    high, low = split(value)
    return jnp.concatenate([high, low, high], axis=axis)


def tripled(constant, size, axis=0):
    parts = []
    for at in range(0, constant.shape[axis], 2 * size):
        high = lax.slice_in_dim(constant, at, at + size, axis=axis)
        low = lax.slice_in_dim(constant, at + size, at + 2 * size, axis=axis)
        parts += [high, high, low]
    return jnp.concatenate(parts, axis=axis)


def side_matrix(rows):
    return ones_where(iota((384, rows.shape[1]), 0) == rows)


def iota(shape, axis):
    return lax.broadcasted_iota(jnp.int32, shape, axis).astype(F32)


def ones_where(condition):
    return jnp.where(condition, 1.0, 0.0).astype(BF16)


def pick(blocks, key):
    chosen = blocks[0]
    for number in range(1, len(blocks)):
        chosen = jnp.where(key == float(number), blocks[number], chosen)
    return chosen


def lane_blocks(value, count):
    return [value[:, 128 * b : 128 * b + 128] for b in range(count)]


def positions(owner):
    records = owner.shape[1]
    column = columns_of(owner)[:, 0:1]
    same = (column == owner) & (iota((records, records), 0) < iota((records, records), 1))
    rank = jnp.sum(jnp.where(same, 1.0, 0.0), axis=0, keepdims=True)
    return owner * 2.0 + rank, column * 2.0 + columns_of(rank)[:, 0:1]


def columns_of(rows):
    count = rows.shape[1]
    eye = ones_where(iota((count, count), 0) == iota((count, count), 1))
    padded = jnp.broadcast_to(rows, (8, count)) if rows.shape[0] == 1 else rows
    return dot_nt(eye, padded.astype(BF16))


def child_table(pool, child_k):
    table = dot(triple(pool), tripled(child_k, 128))
    count = pool.shape[0] // 3
    stacked = [
        jnp.concatenate(
            [table[c * count : (c + 1) * count, o * 128 : o * 128 + 128] for c in range(3)], axis=1
        )
        for o in range(8)
    ]
    high, low = split(jnp.concatenate(stacked, axis=0))
    return jnp.concatenate([high.astype(F32), low.astype(F32)], axis=0).astype(BF16)


def row_picker(key, size):
    if size % 128 == 0:
        hot = ones_where(key == iota((key.shape[0], size), 1))
        return jnp.concatenate([hot, hot], axis=1)
    places = iota((key.shape[0], 2 * size), 1)
    places = jnp.where(places >= float(size), places - float(size), places)
    return ones_where(key == places)


def keys_of(parent, octant, filled):
    own = jnp.where(filled & (parent >= 0.0), octant * float(POOL) + parent, -1.0)
    halo = jnp.where(filled & (parent < 0.0), octant, -1.0)
    return own, halo


def slot_integers(ints, slots, position):
    hot = ones_where(iota((slots, position.shape[1]), 0) == position)
    return dot_nt(hot, ints.astype(BF16))


def requests(ints, pairs, position, scratch):
    records = ints.shape[1]
    scratch[...] = jnp.zeros(scratch.shape, F32)
    scratch[0:8, 0:records] = ints
    scratch[SECOND : SECOND + 8, records : 2 * records] = ints
    places = iota((pairs, records), 0) * 2.0
    hot = jnp.concatenate([ones_where(places == position), ones_where(places + 1.0 == position)], 1)
    return dot_nt(hot, scratch[...].astype(BF16))


def expanded(rows):
    pairs = rows.shape[0]
    slot, pair = iota((2 * pairs, pairs), 0), iota((2 * pairs, pairs), 1)
    hot = [ones_where(slot == 2.0 * pair), ones_where(slot == 2.0 * pair + 1.0)]
    both = jnp.concatenate([rows, pltpu.roll(rows, SECOND, 1)], axis=0).astype(BF16)
    return dot(jnp.concatenate(hot, axis=1), both)


def messages(table, sides, carried):
    faces = dot(table, sides).astype(BF16)
    filled = carried[:, VALID : VALID + 1] > 0.5
    side = carried[:, FSIDE : FSIDE + 1]
    own, halo = keys_of(carried[:, PROW : PROW + 1], carried[:, OCT : OCT + 1], filled)
    face = pick(lane_blocks(dot(row_picker(own, 8 * POOL), faces), 6), side)
    return face, jnp.where(halo >= 0.0, side * 8.0 + halo, -1.0)


def halo_messages(halo_table, sides, keys):
    faces = dot(halo_table, sides)
    rows = [block[8 * h : 8 * h + 8] for h in range(2) for block in lane_blocks(faces, 6)]
    return dot(row_picker(keys, 48), jnp.concatenate(rows, axis=0).astype(BF16))


def determinants(table, halo_table, slope_k, own, halo):
    children = dot(row_picker(own, 8 * POOL), table) + dot(row_picker(halo, 8), halo_table)
    slope_k = tripled(slope_k, 128, 1)
    grads = [dot_nt(slope_k, triple(block)) for block in lane_blocks(children, 3)]
    g = [[grads[c][128 * d : 128 * d + 128] for c in range(3)] for d in range(3)]
    first = g[0][0] * (g[1][1] * g[2][2] - g[2][1] * g[1][2])
    second = g[1][0] * (g[0][1] * g[2][2] - g[2][1] * g[0][2])
    third = g[2][0] * (g[0][1] * g[1][2] - g[1][1] * g[0][2])
    return first - second + third


def coarse_faces(coarse, side_k):
    high, low = split(coarse.T)
    return dot(jnp.concatenate([high, low], axis=0), side_k).astype(BF16)


def coarse_rows(integers, faces):
    filled = integers[:, VALID : VALID + 1] > 0.5
    elem = jnp.where(filled, integers[:, ELEM : ELEM + 1], -1.0)
    hot = row_picker(elem, faces.shape[0] // 2)
    return pick(lane_blocks(dot(hot, faces), 6), integers[:, SIDE : SIDE + 1])


def mortar(fine, coarse, quad, tangent_k):
    parts = [triple(fine)]
    for number in range(4):
        parts.append(triple(jnp.where(quad == float(number), coarse, 0.0)))
    tangents = dot(jnp.concatenate(parts, axis=1), tripled(tangent_k, 128))
    t1, t2 = tangents[:, :128], tangents[:, 128:]
    ahead = lambda value, count: pltpu.roll(value, 128 - 25 * count, 1)
    return ahead(t1, 1) * ahead(t2, 2) - ahead(t1, 2) * ahead(t2, 1)


def partial_sums(normal, integers, back_k, elements):
    slots = integers.shape[0]
    filled = integers[:, VALID : VALID + 1] > 0.5
    side, quad = integers[:, SIDE : SIDE + 1], integers[:, QUAD : QUAD + 1]
    key = side * float(elements) + integers[:, ELEM : ELEM + 1]
    key = jnp.where(filled, key, -1.0)
    parts = []
    for number in range(4):
        parts.append(triple(jnp.where(quad == float(number), normal, 0.0)))
    back = dot(jnp.concatenate(parts, axis=1), tripled(back_k, 128))
    high, low = split(back.T)
    hot = ones_where(key == iota((slots, 6 * elements), 1))
    both = dot(jnp.concatenate([high, low], axis=0), hot)
    return both[:128] + both[128:]


def by_record(slot_rows, places):
    high, low = split(slot_rows)
    hot = ones_where(places == iota((places.shape[0], slot_rows.shape[0]), 1))
    both = dot(hot, jnp.concatenate([high, low], axis=1))
    return both[:, :128] + both[:, 128:]


def fill_pool(pool, last, parents):
    pool[...] = jnp.zeros(pool.shape, F32)
    last[...] = jnp.zeros(last.shape, F32)
    for c in range(3):
        own = parents[c]
        own = own - own[:, MIDDLE : MIDDLE + 1]
        pool[c * POOL : (c + 1) * POOL, 0:125] = own
        last[c : c + 1, 0:125] = own[POOL - 1 :]


def fill_coarse(scratch, coarse):
    for c in range(3):
        scratch[c * 128 + 120 : c * 128 + 128, :] = jnp.zeros((8, coarse.shape[2]), F32)
        whole = coarse[c]
        scratch[c * 128 : c * 128 + 125, :] = whole - whole[MIDDLE : MIDDLE + 1]


def record_integers(parent, octant, elem, side, c_elem, c_side, quad):
    elements = parent.shape[1]
    both = jnp.concatenate([parent, octant, jnp.zeros((6, elements), F32)], axis=0)
    hot = ones_where(iota((elements, elem.shape[1]), 0) == elem)
    chosen = dot(both.astype(BF16), hot)
    rows = [jnp.ones_like(elem), c_elem, c_side, quad, side, chosen[0:1], chosen[1:2],
            jnp.zeros_like(elem)]
    turned = columns_of(both)
    keys = keys_of(turned[:, 0:1], turned[:, 1:2], turned[:, 1:2] >= 0.0)
    return jnp.concatenate(rows, axis=0), keys


def write_partials(partial_out, sums, elements):
    for c in range(3):
        for s in range(6):
            partial_out[c, s * 25 : s * 25 + 25, :] = sums[
                c * 25 : c * 25 + 25, s * elements : (s + 1) * elements
            ]


INPUTS = ("parent", "octant", "elem", "owner", "side", "c_elem", "c_side", "quad", "parents",
          "child_k", "side_k", "coarse", "slope_k", "tangent_k", "back_k")


def kernel(leaves, doms, groups, *refs):
    count = len(INPUTS)
    sources = refs[:count]
    jac_out, normals_out, partial_out = refs[count : count + 3]
    copies = refs[count + 3 : 2 * count + 3]
    (pool, last, halo_in, wide, scratch, ask_send, ask_here, fine_send, fine_here,
     coarse_send, coarse_here,
     in_sems, halo_sems, send_sems, ask_sems, fine_sems, coarse_sems) = refs[2 * count + 3 :]
    leaf, dom = lax.axis_index("leaf"), lax.axis_index("dom")
    ranks = leaves * doms
    me = leaf * doms + dom
    slots = 2 * ranks
    mesh_id = pl.DeviceIdType.MESH

    loads = {
        name: pltpu.make_async_copy(sources[at], copies[at], in_sems.at[at])
        for at, name in enumerate(INPUTS)
    }
    for name in INPUTS:
        loads[name].start()

    def load(name):
        loads[name].wait()
        return copies[INPUTS.index(name)]

    xs = max(doms // 16, 1)
    zs = doms // (2 * xs)
    at_x, at_z, core = dom // (2 * zs), lax.rem(dom // 2, zs), lax.rem(dom, 2)
    z_steps = sorted(range(zs), key=lambda step: -min(step, zs - step))
    by_z = [(step, lax.rem(at_z + step, zs) * 2) for step in z_steps]
    by_core = [(1, 1 - core), (0, core)]

    def others(ahead, act):
        there = lax.rem(leaf + ahead, leaves)

        def plane(step_x, skip):
            base = lax.rem(at_x + step_x, xs) * (2 * zs)
            for step_z, z_part in by_z:
                for step_core, core_part in by_core:
                    if not (skip and step_z == 0 and step_core == 0):
                        act(there, base + z_part + core_part)

        def body(number, carry):
            plane(number + xs // 2, False)
            return carry

        if ahead:
            lax.fori_loop(0, xs, body, 0)
        else:
            for number in range(xs):
                step_x = (number + xs // 2) % xs
                plane(step_x, step_x == 0)

    far_first = sorted(range(leaves), key=lambda step: -min(step, leaves - step))

    barrier = pltpu.get_barrier_semaphore()

    def greet(l, d):
        pl.semaphore_signal(barrier, inc=1, device_id=(l, d), device_id_type=mesh_id)

    for ahead in far_first:
        others(ahead, greet)

    def send_all(ahead, source, target, send_sem, recv_sem):
        def send(l, d):
            pltpu.make_async_remote_copy(
                src_ref=source.at[l * doms + d],
                dst_ref=target.at[me],
                send_sem=send_sem,
                recv_sem=recv_sem,
                device_id=(l, d),
                device_id_type=mesh_id,
            ).start()

        others(ahead, send)

    def wait_rows(ref, rows, sem):
        most = ref.at[pl.ds(0, rows)]
        pltpu.make_async_copy(most, most, sem).wait()

    def wait_leaf(ref, back, sems):
        wait_rows(ref, doms if back else doms - 1, sems.at[back])

    names = ("parent", "octant", "elem", "side", "c_elem", "c_side", "quad")
    ints, keys = record_integers(*[load(name)[...].astype(F32) for name in names])
    position, places = positions(load("owner")[...].astype(F32))
    ask_send[...] = requests(ints, ranks, position, wide).reshape(ask_send.shape)
    fill_pool(pool, last, load("parents"))
    child_k = load("child_k")[...]
    table = child_table(pool[...], child_k)
    sides = side_matrix(load("side_k")[...])

    coarse = load("coarse")
    elements = coarse.shape[2]
    fill_coarse(scratch, coarse)
    faces = coarse_faces(scratch[...], sides)

    pl.semaphore_wait(barrier, ranks - 1)
    after = lax.rem(me + 1, ranks)
    halo = pltpu.make_async_remote_copy(
        src_ref=last,
        dst_ref=halo_in,
        send_sem=halo_sems.at[0],
        recv_sem=halo_sems.at[1],
        device_id=(after // doms, lax.rem(after, doms)),
        device_id_type=mesh_id,
    )
    halo.start()
    for ahead in far_first:
        send_all(ahead, ask_send, ask_here, send_sems.at[0], ask_sems.at[ahead])
    ask_here[pl.ds(me, 1)] = ask_send[pl.ds(me, 1)]
    carried = slot_integers(ints, slots, position)
    fine, fine_keys = messages(table, sides, carried)
    halo.wait()
    halo_table = child_table(jnp.concatenate([halo_in[c : c + 1] for c in range(3)], axis=0), child_k)
    fine = fine + halo_messages(halo_table, sides, fine_keys)
    fine_send[...] = fine.reshape(fine_send.shape)
    for ahead in far_first:
        send_all(ahead, fine_send, fine_here, send_sems.at[1], fine_sems.at[ahead])
    fine_here[pl.ds(me, 1)] = fine_send[pl.ds(me, 1)]

    tangent_k = load("tangent_k")[...]
    back_k = load("back_k")[...]
    slope_k = load("slope_k")[...]

    asked = []
    for group in groups:
        starts = [lax.rem(leaf + leaves - back, leaves) * doms for back in group]
        for back in group:
            wait_leaf(ask_here, back, ask_sems)
        for start in starts:
            rows = ask_here[pl.ds(start, doms)].reshape(doms, 128)
            asked.append(expanded(rows))
        rows = coarse_rows(jnp.concatenate(asked[-len(group) :], axis=0), faces)
        for number, start in enumerate(starts):
            mine = rows[number * 2 * doms : (number + 1) * 2 * doms]
            coarse_send[pl.ds(start, doms)] = mine.reshape(doms, 2, 128)
        for back in group:
            ahead = (leaves - back) % leaves
            send_all(ahead, coarse_send, coarse_here, send_sems.at[2], coarse_sems.at[ahead])
    coarse_here[pl.ds(me, 1)] = coarse_send[pl.ds(me, 1)]

    jac_out[...] = determinants(table, halo_table, slope_k, *keys)[0:125]

    order = [back for group in groups for back in group]
    starts = [lax.rem(leaf + leaves - back, leaves) * doms for back in order]
    part = lambda ref: jnp.concatenate(
        [ref[pl.ds(start, doms)].reshape(2 * doms, 128) for start in starts], axis=0
    )
    for back in order:
        wait_leaf(fine_here, back, fine_sems)
    asked = jnp.concatenate(asked, axis=0)
    normal = mortar(part(fine_here), part(coarse_send), asked[:, QUAD : QUAD + 1], tangent_k)
    write_partials(partial_out, partial_sums(normal, asked, back_k, elements), elements)

    fine = by_record(fine, places)
    quad = columns_of(ints)[:, QUAD : QUAD + 1]
    for back in order:
        wait_leaf(coarse_here, back, coarse_sems)
    coarse = by_record(coarse_here[...].reshape(slots, 128), places)
    turned = mortar(fine, coarse, quad, tangent_k).T
    for c in range(3):
        normals_out[c] = turned[c * 25 : c * 25 + 25]
    for at, ref in enumerate((ask_send, fine_send, coarse_send)):
        wait_rows(ref, ranks - 1, send_sems.at[at])


def store_kernel(*refs):
    count = (len(refs) - 1) // 2
    copies = [
        pltpu.make_async_copy(refs[at], refs[count + at], refs[-1].at[at]) for at in range(count)
    ]
    for copy in copies:
        copy.start()
    for copy in copies:
        copy.wait()


def shards(parents, coarse, parent, octant, elem, side, owner, c_elem, c_side, quad):
    leaves, doms = lax.axis_size("leaf"), lax.axis_size("dom")
    ranks = leaves * doms
    records, elements = elem.shape[0], parent.shape[0]
    row = lambda value: value.reshape(1, -1)
    given = dict(
        parent=row(parent), octant=row(octant), elem=row(elem), side=row(side), owner=row(owner),
        c_elem=row(c_elem), c_side=row(c_side), quad=row(quad),
        parents=parents.transpose(0, 2, 1), coarse=coarse,
        child_k=jnp.asarray(child_constant()), side_k=jnp.asarray(side_constant()),
        slope_k=jnp.asarray(slope_constant()), tangent_k=jnp.asarray(tangent_constant()),
        back_k=jnp.asarray(back_constant()),
    )
    args = [pltpu.with_memory_space_constraint(given[name], pltpu.HBM) for name in INPUTS]
    buffer = pltpu.VMEM((ranks, 2, 128), F32)
    request = pltpu.VMEM((ranks, 1, 128), F32)
    far_first = sorted(range(leaves), key=lambda step: -min(step, leaves - step))
    groups = [far_first[at : at + GROUP] for at in range(0, leaves, GROUP)]
    shapes = (
        jax.ShapeDtypeStruct((125, elements), F32),
        jax.ShapeDtypeStruct((3, 25, records), F32),
        jax.ShapeDtypeStruct((3, 150, coarse.shape[2]), F32),
    )
    results = pl.pallas_call(
        functools.partial(kernel, leaves, doms, groups),
        out_shape=shapes,
        in_specs=[pl.BlockSpec(memory_space=pltpu.HBM)] * len(args),
        out_specs=[pl.BlockSpec(memory_space=pltpu.VMEM)] * 3,
        scratch_shapes=[pltpu.VMEM(arg.shape, arg.dtype) for arg in args] + [
            pltpu.VMEM((3 * POOL, 128), F32),
            pltpu.VMEM((8, 128), F32),
            pltpu.VMEM((8, 128), F32),
            pltpu.VMEM((128, 2 * records), F32),
            pltpu.VMEM((384, coarse.shape[2]), F32),
            request, request, buffer, buffer, buffer, buffer,
            pltpu.SemaphoreType.DMA((len(args),)),
            pltpu.SemaphoreType.DMA((2,)),
            pltpu.SemaphoreType.DMA((3,)),
            pltpu.SemaphoreType.DMA((leaves,)),
            pltpu.SemaphoreType.DMA((leaves,)),
            pltpu.SemaphoreType.DMA((leaves,)),
        ],
        compiler_params=pltpu.CompilerParams(
            collective_id=0, has_side_effects=True, vmem_limit_bytes=40 << 20
        ),
    )(*args)
    return pl.pallas_call(
        store_kernel,
        out_shape=shapes,
        in_specs=[pl.BlockSpec(memory_space=pl.ANY)] * 3,
        out_specs=[pl.BlockSpec(memory_space=pltpu.HBM)] * 3,
        scratch_shapes=[pltpu.SemaphoreType.DMA((3,))],
        compiler_params=pltpu.CompilerParams(vmem_limit_bytes=4 << 20),
    )(*results)


def solution(mesh):
    whole = P(None, None, ("leaf", "dom"))
    line = P(("leaf", "dom"))
    return jax.shard_map(
        shards,
        mesh=mesh,
        in_specs=(whole, whole, line, line, line, line, P(("leaf", "dom"), None), line, line, line),
        out_specs=(P(None, ("leaf", "dom")), whole, whole),
        check_vma=False,
    )
```
